32 devices in a mesh: chan: 16 (over z, x, core), rows: 2 (over y).
Axes of the slice: x: 2, y: 2, z: 4, core: 2. Of those that a mesh axis runs over, the one named last changes fastest.
Arguments:
- image: bfloat16 [768, 1, 32, 128], P('chan', None, 'rows'), may hold values from -3 to 3
- dw_kernel: float32 [768, 7, 7], P('chan'), may hold values from -13 to 13
- ln_gain: float32 [768], P('chan'), may hold values from 0.1 to 1.9
- w_in: bfloat16 [768, 3072], P(None, 'chan'), may hold values from -0.21875 to 0.21875
- w_out: bfloat16 [3072, 768], P('chan'), may hold values from -0.15625 to 0.15625
- layer_scale: float32 [768], P('chan'), may hold values from 0.3 to 1
- cotangent: bfloat16 [768, 1, 32, 128], P('chan', None, 'rows'), may hold values from -6 to 6
Outputs:
- block_out: bfloat16 [768, 1, 32, 128], P('chan', None, 'rows')
- grad_image: bfloat16 [768, 1, 32, 128], P('chan', None, 'rows')
- grad_kernel: float32 [768, 7, 7], P('chan')
- grad_gain: float32 [768], P('chan')
- grad_scale: float32 [768], P('chan')
- grad_w_in: float32 [768, 3072], P(None, 'chan')
- grad_w_out: float32 [3072, 768], P('chan')
The draws below stay inside these ranges and needn't reach their ends.
All inputs are finite; a program needn't handle non-finite values.
Results may differ from the reference program's by a relative error of at most 0.018.
Values may be sent and summed in bfloat16 or wider, within the bound.
A program may use at most 64 MiB of HBM per device.

```python
import math
import jax
import jax.numpy as jnp
from jax import lax

D = 768
HID = 3072
KSIZE = 7
IMGS = 1
WID = 128
HGT = 32
N_CHAN = 16


def draw_dw_kernel(key, part):
    key_scale = jax.random.fold_in(key, 11)
    key_base = jax.random.fold_in(key, 23)
    channel = jnp.arange(D, dtype=jnp.float32)
    ramp = 3.0 ** (channel / (D - 1))
    spread = 10.0 ** jax.random.uniform(key_scale, (D,), jnp.float32, 0.0, 1.0)
    base = jax.random.truncated_normal(key_base, -3.0, 3.0, (D, KSIZE, KSIZE), jnp.float32)
    return (base * (ramp * spread / 7.0)[:, None, None]).astype(jnp.float32)


def with_spikes(drawn, own_key, source, target, shards_of, factor):
    owner, partner = [(jnp.arange(drawn.shape[position]) // (drawn.shape[position] // shards_of)).reshape([-1 if axis == position else 1 for axis in range(drawn.ndim)]) for position in (source, target)]
    chosen = jax.random.permutation(own_key, shards_of)[partner]
    strong = (owner == chosen) | (owner == (partner + shards_of // 2) % shards_of)
    return jnp.where(strong, factor * drawn, drawn)


def level_of(key, extent, pieces, least, largest):
    def one(axis_at, blocks):
        draws = jax.random.uniform(jax.random.fold_in(jax.random.fold_in(key, 6), axis_at), (blocks,), jnp.float32, least / len(pieces), largest / len(pieces))
        return jnp.repeat(jnp.exp(draws), extent[axis_at] // blocks).reshape((-1,) + (1,) * (len(extent) - axis_at - 1))

    gain = one(*pieces[0])
    for cut in pieces[1:]:
        gain = gain * one(*cut)
    return gain


def scatter_about(rng, dims, deviation, limit, shards=(), kind=jnp.bfloat16):
    factor_of = level_of(rng, dims, shards, -0.22, 0.18) if shards else 1.0
    values = jax.random.normal(rng, dims, jnp.float32) * deviation * factor_of
    return jnp.minimum(jnp.maximum(values, -limit), limit).astype(kind)


def heavy_noise(key, extent, scale, reach, cuts, heavy, kind=jnp.bfloat16):
    entries = scale * jax.random.normal(key, extent, jnp.float32)
    if cuts:
        entries = entries * level_of(key, extent, cuts, -0.22, 0.18)
    return jnp.clip(with_spikes(entries, jax.random.fold_in(key, 3), *heavy), -reach, reach).astype(kind)


def setup_inputs(seed: int = 0) -> dict:
    seeds = jax.random.split(jax.random.key(seed), 8)
    image = scatter_about(seeds[0], (D, IMGS, HGT, WID), 0.5, 3.0, ((0, 16), (2, 2)))
    dw_kernel = draw_dw_kernel(jax.random.fold_in(seeds[7], 71), 0)
    ln_gain = jnp.clip(1.0 + 0.18 * jax.random.normal(seeds[2], (D,), jnp.float32), 0.1, 1.9)
    w_in = scatter_about(seeds[3], (D, HID), D ** -0.5, 0.21875, ((1, 16),))
    w_out = heavy_noise(seeds[4], (HID, D), HID ** -0.5, 0.15625, ((0, 16),), (0, 1, 16, 2.0))
    layer_scale = jnp.clip(jnp.exp(math.log(1.0) - 1.2039728 * jax.random.uniform(seeds[5], (D,), jnp.float32) ** level_of(seeds[5], (D,), ((0, 16),), -0.2, 0.2)), 0.3, 1.0)
    cotangent = scatter_about(seeds[6], (D, IMGS, HGT, WID), 1.0, 6.0, ((0, 16), (2, 2)))
    return dict(image=image, dw_kernel=dw_kernel, ln_gain=ln_gain, w_in=w_in, w_out=w_out, layer_scale=layer_scale, cotangent=cotangent)


epsilon = 1e-06
inv_root_two = 0.7071067811865476
inv_root_two_pi = 0.3989422804014327

def gelu_slope(values):
    return 0.5 * (1.0 + lax.erf(values * inv_root_two)) + values * jnp.exp(-0.5 * values * values) * inv_root_two_pi

def forward_taps(padded, kernel, height, breadth):
    running = jnp.zeros((padded.shape[0], padded.shape[1], height, breadth), jnp.float32)
    for u in range(KSIZE):
        for v in range(KSIZE):
            running = running + kernel[:, u, v][:, None, None, None] * padded[:, :, u:u + height, v:v + breadth]
    return running

def transpose_taps(padded, kernel, height, breadth):
    running = jnp.zeros((padded.shape[0], padded.shape[1], height, breadth), jnp.float32)
    for u in range(KSIZE):
        for v in range(KSIZE):
            running = running + kernel[:, u, v][:, None, None, None] * padded[:, :, 6 - u:6 - u + height, 6 - v:6 - v + breadth]
    return running

def correlate_taps(padded, grad, height, breadth):
    columns = []
    for u in range(KSIZE):
        row_terms = []
        for v in range(KSIZE):
            row_terms.append(lax.optimization_barrier(jnp.sum(grad * padded[:, :, u:u + height, v:v + breadth], axis=(1, 2, 3))))
        columns.append(jnp.stack(row_terms, axis=1))
    return jnp.stack(columns, axis=1)

def blocked_sum(weights_blocks, data_blocks):

    def step(running, pair):
        weight_block, data_block = pair
        partial_term = jnp.dot(weight_block, data_block, preferred_element_type=jnp.float32).astype(jnp.bfloat16)
        partial_term = lax.optimization_barrier(partial_term)
        return (running + partial_term.astype(jnp.float32), None)
    start_value = jnp.zeros((weights_blocks.shape[1], data_blocks.shape[2]), jnp.float32)
    result, _ = lax.scan(step, start_value, (weights_blocks, data_blocks))
    return result

def reference(image, dw_kernel, ln_gain, w_in, w_out, layer_scale, cotangent):
    pixels = IMGS * HGT * WID
    hidden_block = HID // N_CHAN
    image_f = image.astype(jnp.float32)
    padded = jnp.pad(image_f, ((0, 0), (0, 0), (3, 3), (3, 3)))
    mixed_in = forward_taps(padded, dw_kernel, HGT, WID).astype(jnp.bfloat16)
    mixed_flat = mixed_in.reshape(D, pixels).astype(jnp.float32)
    centre = lax.optimization_barrier(jnp.mean(mixed_flat, axis=0))
    spread = lax.optimization_barrier(jnp.mean(jnp.square(mixed_flat - centre), axis=0))
    inv_scale = 1.0 / jnp.sqrt(spread + epsilon)
    unit_norm = (mixed_flat - centre) * inv_scale
    normed = (unit_norm * ln_gain[:, None]).astype(jnp.bfloat16)
    pre_act = jnp.dot(w_in.T, normed, preferred_element_type=jnp.float32)
    activated = jax.nn.gelu(pre_act, approximate=False).astype(jnp.bfloat16)
    out_blocks = jnp.transpose(w_out.reshape(N_CHAN, hidden_block, D), (0, 2, 1))
    act_blocks = activated.reshape(N_CHAN, hidden_block, pixels)
    branch = blocked_sum(out_blocks, act_blocks)
    block_out = (image_f.reshape(D, pixels) + layer_scale[:, None] * branch).astype(jnp.bfloat16)
    cotan_flat = cotangent.reshape(D, pixels).astype(jnp.float32)
    scaled = (layer_scale[:, None] * cotan_flat).astype(jnp.bfloat16)
    grad_act = jnp.dot(w_out, scaled, preferred_element_type=jnp.float32)
    grad_w_out = jnp.dot(activated, scaled.T, preferred_element_type=jnp.float32)
    grad_scale = lax.optimization_barrier(jnp.sum(cotan_flat * branch, axis=1))
    grad_pre = (grad_act * gelu_slope(pre_act)).astype(jnp.bfloat16)
    grad_w_in = jnp.dot(normed, grad_pre.T, preferred_element_type=jnp.float32)
    in_blocks = jnp.transpose(w_in.reshape(D, N_CHAN, hidden_block), (1, 0, 2))
    pre_blocks = grad_pre.reshape(N_CHAN, hidden_block, pixels)
    grad_normed = blocked_sum(in_blocks, pre_blocks)
    grad_gain = lax.optimization_barrier(jnp.sum(grad_normed * unit_norm, axis=1))
    scaled_grad = grad_normed * ln_gain[:, None]
    mean_one = lax.optimization_barrier(jnp.mean(scaled_grad, axis=0))
    mean_two = lax.optimization_barrier(jnp.mean(scaled_grad * unit_norm, axis=0))
    grad_mixed = (inv_scale * (scaled_grad - mean_one - unit_norm * mean_two)).astype(jnp.bfloat16)
    grad_four = grad_mixed.reshape(D, IMGS, HGT, WID).astype(jnp.float32)
    grad_padded = jnp.pad(grad_four, ((0, 0), (0, 0), (3, 3), (3, 3)))
    spread_back = transpose_taps(grad_padded, dw_kernel, HGT, WID)
    grad_image = (cotangent.astype(jnp.float32) + spread_back).astype(jnp.bfloat16)
    grad_kernel = correlate_taps(padded, grad_four, HGT, WID)
    return (block_out.reshape(D, IMGS, HGT, WID), grad_image, grad_kernel, grad_gain, grad_scale, grad_w_in, grad_w_out)
```

```python
import functools

import jax
import jax.numpy as jnp
from jax import lax
from jax.experimental import pallas as pl
from jax.experimental.pallas import tpu as pltpu
from jax.sharding import PartitionSpec as P

D = 768
KSIZE = 7
TAPS = KSIZE * KSIZE


epsilon = 1e-06
inv_root_two = 0.7071067811865476
inv_root_two_pi = 0.3989422804014327

GROUP = 4
CUTS = 2
MESH = pl.DeviceIdType.MESH
MIXED, SCALED = 0, 1
NORMED, BRANCH = 0, 1


def shifted(value, shift):
    if shift == 0:
        return value
    breadth = value.shape[1]
    lane = lax.broadcasted_iota(jnp.int32, value.shape, 1)
    rolled = pltpu.roll(value, shift % breadth, 1)
    keep = lane >= shift if shift > 0 else lane < breadth + shift
    return jnp.where(keep, rolled, 0.0)


def flipped(index, bit):
    return index + bit - 2 * bit * lax.rem(lax.div(index, bit), 2)


def block_kernel(
    n,
    rows,
    image_ref,
    cotan_ref,
    taps_ref,
    gain_ref,
    weights_ref,
    block_ref,
    image_grad_ref,
    small_ref,
    grads_ref,
    padded,
    running,
    own,
    gath,
    gain_src,
    gain_in,
    gain_cols,
    w,
    wt,
    ns,
    gact,
    pre,
    ag,
    part_sum,
    red_out,
    red_in,
    piece_in,
    st_out,
    st_in,
    st_all,
    kept,
    sent,
    core_in,
    near_out,
    near_in,
    row_out,
    row_in,
    grad_pad,
    sums_one,
    sums_two,
    image_halo,
    halo_out,
    halo_in,
    small_out,
    small_in,
    a_send,
    g_send,
    g_recv,
    gain_send,
    gain_recv,
    r_send,
    r_recv,
    p_send,
    p_recv,
    s_send,
    s_recv,
    t_send,
    t_recv,
    pair_send,
    pair_recv,
):
    f32, bf16 = jnp.float32, jnp.bfloat16
    me = lax.axis_index("chan")
    row = lax.axis_index("rows")
    plane, lane = lax.div(me, GROUP), lax.rem(me, GROUP)
    height, channels, breadth = image_ref.shape
    planes = n // GROUP
    part = height // GROUP
    pc = part // CUTS
    hidden = weights_ref.shape[1]
    width = weights_ref.shape[2]
    band = GROUP * channels
    steps = row_out.shape[0]
    groups = channels // 8
    up, down = lax.rem(row + rows - 1, rows), lax.rem(row + 1, rows)
    partners = [flipped(row, 2**s) for s in range(steps)]

    barrier = pltpu.get_barrier_semaphore()
    for k in range(1, n):
        pl.semaphore_signal(
            barrier, inc=1, device_id={"chan": lax.rem(me + k, n)}, device_id_type=MESH
        )
    for other in [up, down] + partners:
        pl.semaphore_signal(barrier, inc=1, device_id={"rows": other}, device_id_type=MESH)

    def remote(source, target, send, recv, device):
        return pltpu.make_async_remote_copy(
            src_ref=source,
            dst_ref=target,
            send_sem=send,
            recv_sem=recv,
            device_id=device,
            device_id_type=MESH,
        )

    def pair(index, source, target, device):
        copy = remote(source, target, pair_send.at[index], pair_recv.at[index], device)
        copy.start()
        return copy

    def mate(k):
        return lax.rem(lane + k, GROUP)


    def spread_copy(a, h, k):
        lines = pl.ds(mate(k) * part + h * pc, pc)
        return remote(
            own.at[a, lines],
            gath.at[a, h, me],
            a_send.at[a, h, k],
            g_recv.at[a, h, me],
            {"chan": plane * GROUP + mate(k)},
        )

    def hop_copy(a, h, s, side):
        return remote(
            gath.at[a, h, s],
            gath.at[a, h, s],
            g_send.at[a, h, side, s],
            g_recv.at[a, h, s],
            {"chan": me + GROUP if side == 0 else me - GROUP},
        )

    to_right, to_left = plane + 1 < planes, plane >= 1

    def pass_on(a, h, s, side):
        @pl.when(to_right if side == 0 else to_left)
        def _():
            hop_copy(a, h, s, side).start()

    def hop_first(a, h, q):
        s = plane * GROUP + mate(q)
        if not (isinstance(q, int) and q == 0):
            hop_copy(a, h, s, 0).wait_recv()
        pass_on(a, h, s, 0)
        pass_on(a, h, s, 1)

    def hop(a, h, t, q):
        @pl.when(plane >= t)
        def _():
            s = (plane - t) * GROUP + mate(q)
            hop_copy(a, h, s, 0).wait_recv()
            pass_on(a, h, s, 0)

        @pl.when(plane + t < planes)
        def _():
            s = (plane + t) * GROUP + mate(q)
            hop_copy(a, h, s, 1).wait_recv()
            pass_on(a, h, s, 1)

    def hops(a, t, h):
        @pl.loop(0, GROUP)
        def _(q):
            hop(a, h, t, q)

    def begin(a):
        for h in range(CUTS):
            for k in range(1, GROUP):
                spread_copy(a, h, k).start()
            hop_first(a, h, 0)

    def firsts(a):
        for h in range(CUTS):

            @pl.loop(1, GROUP)
            def _(q):
                hop_first(a, h, q)


    scale = jnp.broadcast_to(taps_ref[:, TAPS + 1 : TAPS + 2], (channels, breadth))
    gain = jnp.broadcast_to(taps_ref[:, TAPS : TAPS + 1], (channels, breadth))

    @pl.loop(0, height)
    def _(r):
        padded[r + 3] = image_ref[r].astype(f32)
        own[SCALED, r] = (scale * cotan_ref[r].astype(f32)).astype(bf16)

    gain_src[...] = gain_ref[...]

    def keep_own(a):
        for h in range(CUTS):
            for i in range(pc):
                gath[a, h, me, i] = own[a, lane * part + h * pc + i]

    keep_own(SCALED)
    pl.semaphore_wait(barrier, n + 1 + steps)

    image_halos = [
        pair(0, image_ref.at[pl.ds(0, 3)], image_halo.at[1], {"rows": up}),
        pair(1, image_ref.at[pl.ds(height - 3, 3)], image_halo.at[0], {"rows": down}),
    ]
    begin(SCALED)

    def block(a, index):
        return w.at[a, pl.ds(index * hidden, hidden)]

    near_w, core_w, far_w = [None] * 2, [None] * 2, [None] * 2
    near_w[1] = pair(2, weights_ref.at[1], block(1, 1), {"chan": flipped(me, 2)})
    for a in range(2):
        core_w[a] = pair(3 + a, weights_ref.at[a], block(a, 2), {"chan": flipped(me, 1)})

    def gain_copy(k):
        return remote(
            gain_src,
            gain_in.at[me],
            gain_send.at[k],
            gain_recv.at[me],
            {"chan": lax.rem(me + k, n)},
        )

    @pl.loop(1, n)
    def _(k):
        gain_copy(k).start()

    gain_in[me] = gain_ref[...]
    for a in range(2):
        w[a, pl.ds(0, hidden)] = weights_ref[a]

    for copy in image_halos:
        copy.wait()
    above = jnp.where(row > 0, 1.0, 0.0).astype(f32)
    below = jnp.where(row < rows - 1, 1.0, 0.0).astype(f32)
    for i in range(3):
        padded[i] = image_halo[0, i].astype(f32) * above
        padded[height + 3 + i] = image_halo[1, i].astype(f32) * below

    firsts(SCALED)

    def spaced(g, count, first):
        span = groups - first
        low = jnp.maximum(lax.div((g - first) * count, span), 0)
        high = jnp.maximum(lax.div((g + 1 - first) * count, span), 0)
        return jnp.where(g < first, 0, low), jnp.where(g < first, 0, high)

    @pl.loop(0, groups)
    def _(g):
        group = pl.ds(pl.multiple_of(8 * g, 8), 8)
        taps = taps_ref[group, :]
        sums = [None] * height
        for v in range(KSIZE):
            shifts = [shifted(padded[r, group, :], 3 - v) for r in range(height + 6)]
            for u in range(KSIZE):
                t = u * KSIZE + v
                tap = jnp.broadcast_to(taps[:, t : t + 1], taps.shape)
                for r in range(height):
                    term = tap * shifts[r + u]
                    sums[r] = term if sums[r] is None else sums[r] + term
        for r in range(height):
            running[r, group, :] = sums[r]
        low, high = spaced(g, CUTS * GROUP, groups // 2)

        @pl.loop(low, high)
        def _(e):
            hop(SCALED, lax.div(e, GROUP), 1, lax.rem(e, GROUP))

    @pl.loop(0, height)
    def _(r):
        own[MIXED, r] = running[r].astype(bf16)

    keep_own(MIXED)
    begin(MIXED)
    near_w[0] = pair(5, weights_ref.at[0], block(0, 1), {"chan": flipped(me, 2)})
    for h in range(CUTS):
        hops(SCALED, 2, h)
    firsts(MIXED)

    @pl.loop(3, planes)
    def _(t):
        for h in range(CUTS):
            hops(SCALED, t, h)
        for h in range(CUTS):
            hops(MIXED, t - 2, h)

    def far(a):
        near_w[a].wait()
        far_w[a] = pair(6 + a, block(a, 1), block(a, 3), {"chan": flipped(me, 1)})

    far(1)

    def columns(i):
        return pl.ds(pl.multiple_of(i * breadth, breadth), breadth)

    for h in range(CUTS):

        @pl.loop(0, pc)
        def _(i):
            for s in range(0, n, 2):
                both = [gath[SCALED, h, s + k, i].astype(f32) for k in range(2)]
                ns[1, h, pl.ds(s * channels, 2 * channels), columns(i)] = jnp.concatenate(
                    both, axis=0
                ).astype(bf16)

    @pl.loop(1, n)
    def _(k):
        copy = remote(
            gain_src,
            gain_in.at[lax.rem(me + n - k, n)],
            gain_send.at[k],
            gain_recv.at[lax.rem(me + n - k, n)],
            {"chan": lax.rem(me + k, n)},
        )
        copy.wait()

    @pl.loop(0, n)
    def _(s):
        square = jnp.broadcast_to(gain_in[s], (breadth, breadth)).T
        gain_cols[s] = square[:channels]

    for h in range(CUTS):
        hops(MIXED, planes - 2, h)
    core_w[1].wait()
    far_w[1].wait()
    double = 2 * hidden

    def half(index):
        return pl.ds(pl.multiple_of(index * double, double), double)

    for h in range(CUTS):

        @pl.loop(0, GROUP // 2)
        def _(index):
            gact[h, half(index)] = jnp.dot(
                w[1, half(index)], ns[1, h], preferred_element_type=f32
            )

    far(0)

    def turn(a):
        @pl.loop(0, GROUP * hidden // 128)
        def _(j):
            piece = pl.ds(pl.multiple_of(j * 128, 128), 128)
            wt[a, :, piece] = w[a, piece, :].T

    turn(1)
    core_w[0].wait()
    far_w[0].wait()
    turn(0)


    def normalized(h):
        @pl.loop(0, pc)
        def _(i):
            total = gath[MIXED, h, 0, i].astype(f32)
            for s in range(1, n):
                total += gath[MIXED, h, s, i].astype(f32)
            centre = jnp.sum(total, axis=0, keepdims=True) * (1.0 / D)
            total = jnp.zeros((channels, breadth), f32)
            for s in range(n):
                total += jnp.square(gath[MIXED, h, s, i].astype(f32) - centre)
            spread = jnp.sum(total, axis=0, keepdims=True) * (1.0 / D)
            inv_scale = lax.rsqrt(spread + epsilon)
            st_out[h * pc + i, 2:3] = centre
            st_out[h * pc + i, 3:4] = inv_scale
            for s in range(0, n, 2):
                both = [
                    (gath[MIXED, h, s + k, i].astype(f32) - centre) * inv_scale * gain_cols[s + k]
                    for k in range(2)
                ]
                ns[0, h, pl.ds(s * channels, 2 * channels), columns(i)] = jnp.concatenate(
                    both, axis=0
                ).astype(bf16)

    def activate(h):
        @pl.loop(0, GROUP // 2)
        def _(index):
            pre[half(index)] = jnp.dot(w[0, half(index)], ns[0, h], preferred_element_type=f32)

        @pl.loop(0, GROUP * hidden // 32)
        def _(j):
            lines = pl.ds(pl.multiple_of(j * 32, 32), 32)
            value = pre[lines]
            cdf = 0.5 * (1.0 + lax.erf(value * inv_root_two))
            slope = cdf + value * jnp.exp(-0.5 * value * value) * inv_root_two_pi
            ag[1, h, lines] = (value * cdf).astype(bf16)
            ag[0, h, lines] = (gact[h, lines] * slope).astype(bf16)

    def sum_copy(a, h, p, side):
        target = p if side == 0 else jnp.where(p == plane - 1, planes, p)
        return remote(
            red_out.at[a, h, p],
            red_in.at[a, h, target],
            r_send.at[a, h, p],
            r_recv.at[a, h, target],
            {"chan": me + GROUP if side == 0 else me - GROUP},
        )

    def round_out(a, h, p):
        @pl.loop(0, GROUP)
        def _(q):
            for i in range(pc):
                red_out[a, h, p, q, i] = part_sum[a, h, p, q, i].astype(bf16)

    def take(a, h, p, index):
        copy = remote(
            red_out.at[a, h, p],
            red_in.at[a, h, index],
            r_send.at[a, h, p],
            r_recv.at[a, h, index],
            {"chan": lax.rem(me + GROUP, n)},
        )
        copy.wait_recv()

        @pl.loop(0, GROUP)
        def _(q):
            for i in range(pc):
                part_sum[a, h, p, q, i] += red_in[a, h, index, q, i].astype(f32)

    def partial(a, h):
        @pl.loop(0, planes)
        def _(j):
            p = jnp.where(plane < planes // 2, planes - 1 - j, j)
            lines = pl.ds(pl.multiple_of(p * band, band), band)
            result = jnp.dot(wt[a, lines], ag[a, h], preferred_element_type=f32)
            for q in range(GROUP):
                for i in range(pc):
                    part_sum[a, h, p, q, i] = result[
                        q * channels : (q + 1) * channels, i * breadth : (i + 1) * breadth
                    ]

            @pl.when((plane == 0) & (p > 0))
            def _():
                round_out(a, h, p)
                sum_copy(a, h, p, 0).start()

            @pl.when((plane == planes - 1) & (p < plane))
            def _():
                round_out(a, h, p)
                sum_copy(a, h, p, 1).start()

    def relay(a, h, tau):
        right = planes - 1 - tau + plane

        @pl.when((plane > 0) & (right < planes))
        def _():
            take(a, h, right, right)
            round_out(a, h, right)
            sum_copy(a, h, right, 0).start()

        left = tau - (planes - 1 - plane)

        @pl.when((plane < planes - 1) & (left >= 0))
        def _():
            take(a, h, left, left)
            round_out(a, h, left)
            sum_copy(a, h, left, 1).start()

    def piece_copy(a, h, k):
        return remote(
            red_out.at[a, h, plane, mate(k)],
            piece_in.at[a, pl.ds(lane * part + h * pc, pc)],
            p_send.at[a, h, k],
            p_recv.at[a, h, lane],
            {"chan": plane * GROUP + mate(k)},
        )

    def finals(a, h):
        @pl.when(plane > 0)
        def _():
            take(a, h, plane, plane)

        @pl.when(plane < planes - 1)
        def _():
            take(a, h, plane, planes)

        round_out(a, h, plane)
        for k in range(1, GROUP):
            piece_copy(a, h, k).start()
        for i in range(pc):
            piece_in[a, lane * part + h * pc + i] = red_out[a, h, plane, lane, i]

    def pieces(a, h):
        for k in range(1, GROUP):
            source = mate(GROUP - k)
            copy = remote(
                red_out.at[a, h, plane, mate(k)],
                piece_in.at[a, pl.ds(source * part + h * pc, pc)],
                p_send.at[a, h, k],
                p_recv.at[a, h, source],
                {"chan": plane * GROUP + mate(k)},
            )
            copy.wait()

    def stats_copy(h, k):
        other = lax.rem(plane + k, planes)
        return remote(
            st_out.at[pl.ds(h * pc, pc)],
            st_in.at[plane, pl.ds(h * pc, pc)],
            s_send.at[h, k],
            s_recv.at[h, plane],
            {"chan": other * GROUP + lane},
        )

    def stats(h):
        @pl.loop(0, pc)
        def _(i):
            centre, inv_scale = st_out[h * pc + i, 2:3], st_out[h * pc + i, 3:4]
            one = jnp.zeros((channels, breadth), f32)
            two = jnp.zeros((channels, breadth), f32)
            for s in range(n):
                gained = part_sum[NORMED, h, s // GROUP, s % GROUP, i] * gain_cols[s]
                one += gained
                two += gained * ((gath[MIXED, h, s, i].astype(f32) - centre) * inv_scale)
            st_out[h * pc + i, 0:1] = jnp.sum(one, axis=0, keepdims=True)
            st_out[h * pc + i, 1:2] = jnp.sum(two, axis=0, keepdims=True)

        for k in range(1, planes):
            stats_copy(h, k).start()

    def stats_total(h):
        for k in range(1, planes):
            source = lax.rem(plane + planes - k, planes)
            copy = remote(
                st_out.at[pl.ds(h * pc, pc)],
                st_in.at[source, pl.ds(h * pc, pc)],
                s_send.at[h, k],
                s_recv.at[h, source],
                {"chan": lax.rem(plane + k, planes) * GROUP + lane},
            )
            copy.wait()
        for i in range(pc):
            here = h * pc + i
            total = st_out[here]
            for k in range(1, planes):
                total += st_in[lax.rem(plane + k, planes), here]
            line = lane * part + here
            st_all[line, 0:2] = total[0:2]
            st_all[line, 2:4] = st_out[here, 2:4]
        for k in range(1, GROUP):
            lines = pl.ds(lane * part + h * pc, pc)
            remote(
                st_all.at[lines],
                st_all.at[lines],
                t_send.at[h, k],
                t_recv.at[h, lane],
                {"chan": plane * GROUP + mate(k)},
            ).start()

    def stats_pieces(h):
        for k in range(1, GROUP):
            source = mate(GROUP - k)
            copy = remote(
                st_all.at[pl.ds(lane * part + h * pc, pc)],
                st_all.at[pl.ds(source * part + h * pc, pc)],
                t_send.at[h, k],
                t_recv.at[h, source],
                {"chan": plane * GROUP + mate(k)},
            )
            copy.wait()

    contract_tail = (((1,), (1,)), ((), ()))

    def weight_grad(a, index):
        lines = pl.ds(index * hidden, hidden)
        total = lax.dot_general(
            ag[a, 0, lines], ns[a, 0], contract_tail, preferred_element_type=f32
        )
        for h in range(1, CUTS):
            total += lax.dot_general(
                ag[a, h, lines], ns[a, h], contract_tail, preferred_element_type=f32
            )
        return total

    for h in range(CUTS):
        hops(MIXED, planes - 1, h)
        normalized(h)
        activate(h)
        partial(NORMED, h)
    for h in range(CUTS):
        stats(h)

    core = [None] * 2
    for a in range(2):
        for index in range(2):
            sent[a, pl.ds(index * hidden, hidden)] = weight_grad(a, 2 + index).astype(bf16)
        core[a] = pair(8 + a, sent.at[a], core_in.at[a], {"chan": flipped(me, 1)})
    for h in range(CUTS):
        relay(NORMED, h, 1)
    for a in range(2):
        for index in range(2):
            kept[a, pl.ds(index * hidden, hidden)] = weight_grad(a, index)
    partial(BRANCH, 0)

    @pl.loop(2, planes - 1)
    def _(tau):
        for h in range(CUTS):
            relay(NORMED, h, tau)

    for h in range(1, CUTS):
        partial(BRANCH, h)
    for h in range(CUTS):
        stats_total(h)

    near = [None] * 2
    for a in range(2):
        core[a].wait()

        @pl.loop(0, hidden // 16)
        def _(i):
            mine = pl.ds(pl.multiple_of(16 * i, 16), 16)
            other = pl.ds(pl.multiple_of(hidden + 16 * i, 16), 16)
            grads_ref[a, mine, :] = kept[a, mine, :] + core_in[a, mine, :].astype(f32)
            near_out[a, mine, :] = (kept[a, other, :] + core_in[a, other, :].astype(f32)).astype(
                bf16
            )

        near[a] = pair(10 + a, near_out.at[a], near_in.at[a], {"chan": flipped(me, 2)})

    for h in range(CUTS):
        finals(NORMED, h)

    def row_step(a, s):
        return pair(
            14 + 2 * s + a, row_out.at[s, a], row_in.at[s, a], {"rows": partners[s]}
        )

    row_copies = [None] * 2

    def row_begin(a):
        near[a].wait()

        @pl.loop(0, hidden // 16)
        def _(i):
            mine = pl.ds(pl.multiple_of(16 * i, 16), 16)
            row_out[0, a, mine, :] = (
                grads_ref[a, mine, :] + near_in[a, mine, :].astype(f32)
            ).astype(bf16)

        row_copies[a] = row_step(a, 0)

    row_begin(0)
    for h in range(CUTS):
        stats_pieces(h)
        pieces(NORMED, h)

    sums_one[...] = jnp.zeros_like(sums_one)
    sums_two[...] = jnp.zeros_like(sums_two)

    def normalize(start, stop):
        @pl.loop(start, stop)
        def _(r):
            grad_normed = piece_in[NORMED, r].astype(f32)
            line = st_all[r]
            centre, inv_scale = line[2:3], line[3:4]
            unit = (own[MIXED, r].astype(f32) - centre) * inv_scale
            sums_one[...] += grad_normed * unit
            scaled_grad = grad_normed * gain
            mixed_grad = inv_scale * (
                scaled_grad - line[0:1] * (1.0 / D) - unit * (line[1:2] * (1.0 / D))
            )
            grad_pad[r + 3] = mixed_grad.astype(bf16).astype(f32)

    normalize(0, 3)
    normalize(height - 3, height)
    for i in range(3):
        halo_out[0, i] = grad_pad[3 + i].astype(bf16)
        halo_out[1, i] = grad_pad[height + i].astype(bf16)
    halos = [
        pair(12, halo_out.at[0], halo_in.at[1], {"rows": up}),
        pair(13, halo_out.at[1], halo_in.at[0], {"rows": down}),
    ]
    normalize(3, height - 3)
    row_begin(1)
    for copy in halos:
        copy.wait()
    for i in range(3):
        grad_pad[i] = halo_in[0, i].astype(f32) * above
        grad_pad[height + 3 + i] = halo_in[1, i].astype(f32) * below

    events = (planes - 2) * CUTS

    @pl.loop(0, groups)
    def _(g):
        group = pl.ds(pl.multiple_of(8 * g, 8), 8)
        taps = taps_ref[group, :]
        position = lax.broadcasted_iota(jnp.int32, taps.shape, 1)
        taps_grad = jnp.zeros_like(taps)
        sums = [None] * height
        for v in range(KSIZE):
            shifts = [shifted(grad_pad[r, group, :], v - 3) for r in range(height + 6)]
            for u in range(KSIZE):
                t = u * KSIZE + v
                tap = jnp.broadcast_to(taps[:, t : t + 1], taps.shape)
                for r in range(height):
                    term = tap * shifts[r + 6 - u]
                    sums[r] = term if sums[r] is None else sums[r] + term
                both = [shifts[r + 3] * padded[r + u, group, :] for r in range(height)]
                while len(both) > 1:
                    both = [p + q for p, q in zip(both[::2], both[1::2])] + both[
                        len(both) // 2 * 2 :
                    ]
                taps_grad = jnp.where(
                    position == t, jnp.sum(both[0], axis=1, keepdims=True), taps_grad
                )
        for r in range(height):
            running[r, group, :] = sums[r]
        small_ref[group, :] = taps_grad
        low, high = spaced(g, events, 0)

        @pl.loop(low, high)
        def _(e):
            relay(BRANCH, lax.rem(e, CUTS), 1 + lax.div(e, CUTS))

    for h in range(CUTS):
        finals(BRANCH, h)

    @pl.loop(0, height)
    def _(r):
        image_grad_ref[r] = (running[r] + cotan_ref[r].astype(f32)).astype(bf16)

    for s in range(steps):
        for a in range(2):
            row_copies[a].wait()
            final = s == steps - 1

            @pl.loop(0, hidden // 16)
            def _(i):
                mine = pl.ds(pl.multiple_of(16 * i, 16), 16)
                total = row_out[s, a, mine, :].astype(f32) + row_in[s, a, mine, :].astype(f32)
                if final:
                    grads_ref[a, mine, :] = total
                else:
                    row_out[s + 1, a, mine, :] = total.astype(bf16)

            if not final:
                row_copies[a] = row_step(a, s + 1)

    for h in range(CUTS):
        pieces(BRANCH, h)

    @pl.loop(0, height)
    def _(r):
        branch = piece_in[BRANCH, r].astype(f32)
        sums_two[...] += branch * cotan_ref[r].astype(f32)
        block_ref[r] = (image_ref[r].astype(f32) + scale * branch).astype(bf16)

    position = lax.broadcasted_iota(jnp.int32, small_ref.shape, 1)
    small = small_ref[...]
    small = jnp.where(position == TAPS, jnp.sum(sums_one[...], axis=1, keepdims=True), small)
    small = jnp.where(position == TAPS + 1, jnp.sum(sums_two[...], axis=1, keepdims=True), small)
    for s in range(steps):
        small_out[s] = small
        step = pair(
            14 + 2 * steps + s, small_out.at[s], small_in.at[s], {"rows": partners[s]}
        )
        step.wait()
        small = small + small_in[s]
    small_ref[...] = small


    for copy in [core_w[0], core_w[1]]:
        pass
    for a in range(2):
        for h in range(CUTS):
            for k in range(1, GROUP):
                spread_copy(a, h, k).wait_send()

            @pl.loop(0, n)
            def _(s):
                home = lax.div(s, GROUP)

                @pl.when(to_right & (home <= plane))
                def _():
                    hop_copy(a, h, s, 0).wait_send()

                @pl.when(to_left & (home >= plane))
                def _():
                    hop_copy(a, h, s, 1).wait_send()

            @pl.loop(0, planes)
            def _(p):
                @pl.when(p > plane)
                def _():
                    sum_copy(a, h, p, 0).wait_send()

                @pl.when(p < plane)
                def _():
                    sum_copy(a, h, p, 1).wait_send()


def run_block(n, arrays):
    f32, bf16 = jnp.float32, jnp.bfloat16
    height, channels, breadth = arrays[0].shape
    hidden, width = arrays[4].shape[1:]
    planes = n // GROUP
    part = height // GROUP
    pc = part // CUTS
    every = GROUP * hidden
    pixels = pc * breadth
    rows = lax.axis_size("rows")
    steps = rows.bit_length() - 1
    pairs = 14 + 3 * steps
    vmem = pl.BlockSpec(memory_space=pltpu.VMEM)
    dma = pltpu.SemaphoreType.DMA
    return pl.pallas_call(
        functools.partial(block_kernel, n, rows),
        out_shape=(
            jax.ShapeDtypeStruct((height, channels, breadth), bf16),
            jax.ShapeDtypeStruct((height, channels, breadth), bf16),
            jax.ShapeDtypeStruct((channels, 128), f32),
            jax.ShapeDtypeStruct((2, hidden, width), f32),
        ),
        in_specs=[vmem] * 5,
        out_specs=(vmem, vmem, vmem, vmem),
        scratch_shapes=[
            pltpu.VMEM((height + 6, channels, breadth), f32),
            pltpu.VMEM((height, channels, breadth), f32),
            pltpu.VMEM((2, height, channels, breadth), bf16),
            pltpu.VMEM((2, CUTS, n, pc, channels, breadth), bf16),
            pltpu.VMEM((1, 128), f32),
            pltpu.VMEM((n, 1, 128), f32),
            pltpu.VMEM((n, channels, breadth), f32),
            pltpu.VMEM((2, every, width), bf16),
            pltpu.VMEM((2, width, every), bf16),
            pltpu.VMEM((2, CUTS, width, pixels), bf16),
            pltpu.VMEM((CUTS, every, pixels), f32),
            pltpu.VMEM((every, pixels), f32),
            pltpu.VMEM((2, CUTS, every, pixels), bf16),
            pltpu.VMEM((2, CUTS, planes, GROUP, pc, channels, breadth), f32),
            pltpu.VMEM((2, CUTS, planes, GROUP, pc, channels, breadth), bf16),
            pltpu.VMEM((2, CUTS, planes + 1, GROUP, pc, channels, breadth), bf16),
            pltpu.VMEM((2, height, channels, breadth), bf16),
            pltpu.VMEM((part, 4, breadth), f32),
            pltpu.VMEM((planes, part, 4, breadth), f32),
            pltpu.VMEM((height, 4, breadth), f32),
            pltpu.VMEM((2, 2 * hidden, width), f32),
            pltpu.VMEM((2, 2 * hidden, width), bf16),
            pltpu.VMEM((2, 2 * hidden, width), bf16),
            pltpu.VMEM((2, hidden, width), bf16),
            pltpu.VMEM((2, hidden, width), bf16),
            pltpu.VMEM((steps, 2, hidden, width), bf16),
            pltpu.VMEM((steps, 2, hidden, width), bf16),
            pltpu.VMEM((height + 6, channels, breadth), f32),
            pltpu.VMEM((channels, breadth), f32),
            pltpu.VMEM((channels, breadth), f32),
            pltpu.VMEM((2, 3, channels, breadth), bf16),
            pltpu.VMEM((2, 3, channels, breadth), bf16),
            pltpu.VMEM((2, 3, channels, breadth), bf16),
            pltpu.VMEM((steps, channels, 128), f32),
            pltpu.VMEM((steps, channels, 128), f32),
            dma((2, CUTS, GROUP)),
            dma((2, CUTS, 2, n)),
            dma((2, CUTS, n)),
            dma((n,)),
            dma((n,)),
            dma((2, CUTS, planes)),
            dma((2, CUTS, planes + 1)),
            dma((2, CUTS, GROUP)),
            dma((2, CUTS, GROUP)),
            dma((CUTS, planes)),
            dma((CUTS, planes)),
            dma((CUTS, GROUP)),
            dma((CUTS, GROUP)),
            dma((pairs,)),
            dma((pairs,)),
        ],
        compiler_params=pltpu.CompilerParams(
            collective_id=0, has_side_effects=True, vmem_limit_bytes=52 * 2**20
        ),
        cost_estimate=pl.CostEstimate(
            flops=4000000000, bytes_accessed=10000000, transcendentals=0
        ),
    )(*arrays)


def body(image, dw_kernel, ln_gain, w_in, w_out, layer_scale, cotangent):
    channels = image.shape[0]
    n = lax.axis_size("chan")
    image_rows = jnp.transpose(image[:, 0], (1, 0, 2))
    cotan_rows = jnp.transpose(cotangent[:, 0], (1, 0, 2))
    taps = jnp.concatenate(
        [
            dw_kernel.reshape(channels, TAPS),
            ln_gain[:, None],
            layer_scale[:, None],
            jnp.zeros((channels, 128 - TAPS - 2), jnp.float32),
        ],
        axis=1,
    )
    gain_row = jnp.pad(ln_gain[None, :], ((0, 0), (0, 128 - channels)))
    block_out, image_grad, small, grads = run_block(
        n, (image_rows, cotan_rows, taps, gain_row, jnp.stack([w_in.T, w_out]))
    )
    return (
        jnp.transpose(block_out, (1, 0, 2))[:, None],
        jnp.transpose(image_grad, (1, 0, 2))[:, None],
        small[:, :TAPS].reshape(channels, KSIZE, KSIZE),
        small[:, TAPS],
        small[:, TAPS + 1],
        grads[0].T,
        grads[1],
    )


def solution(mesh):
    return jax.shard_map(
        body,
        mesh=mesh,
        in_specs=(
            P("chan", None, "rows", None),
            P("chan", None, None),
            P("chan"),
            P(None, "chan"),
            P("chan", None),
            P("chan"),
            P("chan", None, "rows", None),
        ),
        out_specs=(
            P("chan", None, "rows", None),
            P("chan", None, "rows", None),
            P("chan", None, None),
            P("chan"),
            P("chan"),
            P(None, "chan"),
            P("chan", None),
        ),
        check_vma=False,
    )
```

```python
import functools

import jax
import jax.numpy as jnp
from jax import lax
from jax.experimental import pallas as pl
from jax.experimental.pallas import tpu as pltpu
from jax.sharding import PartitionSpec as P

D = 768
KSIZE = 7
TAPS = KSIZE * KSIZE


epsilon = 1e-06
inv_root_two = 0.7071067811865476
inv_root_two_pi = 0.3989422804014327

GROUP = 4
CUTS = 2
MESH = pl.DeviceIdType.MESH
MIXED, SCALED = 0, 1
NORMED, BRANCH = 0, 1


def shifted(value, shift):
    if shift == 0:
        return value
    breadth = value.shape[1]
    lane = lax.broadcasted_iota(jnp.int32, value.shape, 1)
    rolled = pltpu.roll(value, shift % breadth, 1)
    keep = lane >= shift if shift > 0 else lane < breadth + shift
    return jnp.where(keep, rolled, 0.0)


def flipped(index, bit):
    return index + bit - 2 * bit * lax.rem(lax.div(index, bit), 2)


def block_kernel(
    n,
    rows,
    image_ref,
    cotan_ref,
    taps_ref,
    gain_ref,
    weights_ref,
    block_ref,
    image_grad_ref,
    small_ref,
    grads_ref,
    padded,
    running,
    own,
    gath,
    gain_src,
    gain_in,
    gain_cols,
    w,
    wt,
    ns,
    gact,
    pre,
    ag,
    part_sum,
    red_out,
    red_in,
    piece_in,
    st_out,
    st_in,
    st_all,
    kept,
    sent,
    core_in,
    near_out,
    near_in,
    row_out,
    row_in,
    grad_pad,
    sums_one,
    sums_two,
    products,
    image_halo,
    halo_out,
    halo_in,
    small_out,
    small_in,
    a_send,
    g_send,
    g_recv,
    gain_send,
    gain_recv,
    r_send,
    r_recv,
    p_send,
    p_recv,
    s_send,
    s_recv,
    t_send,
    t_recv,
    pair_send,
    pair_recv,
):
    f32, bf16 = jnp.float32, jnp.bfloat16
    me = lax.axis_index("chan")
    row = lax.axis_index("rows")
    plane, lane = lax.div(me, GROUP), lax.rem(me, GROUP)
    height, channels, breadth = image_ref.shape
    planes = n // GROUP
    part = height // GROUP
    pc = part // CUTS
    hidden = weights_ref.shape[1]
    width = weights_ref.shape[2]
    band = GROUP * channels
    steps = row_out.shape[0]
    groups = channels // 8
    up, down = lax.rem(row + rows - 1, rows), lax.rem(row + 1, rows)
    partners = [flipped(row, 2**s) for s in range(steps)]

    barrier = pltpu.get_barrier_semaphore()
    for k in range(1, n):
        pl.semaphore_signal(
            barrier, inc=1, device_id={"chan": lax.rem(me + k, n)}, device_id_type=MESH
        )
    for other in [up, down] + partners:
        pl.semaphore_signal(barrier, inc=1, device_id={"rows": other}, device_id_type=MESH)

    def remote(source, target, send, recv, device):
        return pltpu.make_async_remote_copy(
            src_ref=source,
            dst_ref=target,
            send_sem=send,
            recv_sem=recv,
            device_id=device,
            device_id_type=MESH,
        )

    def pair(index, source, target, device):
        copy = remote(source, target, pair_send.at[index], pair_recv.at[index], device)
        copy.start()
        return copy

    def mate(k):
        return flipped(flipped(lane, 1), 2) if k == 3 else flipped(lane, k) if k else lane


    def spread_copy(a, h, k):
        lines = pl.ds(mate(k) * part + h * pc, pc)
        return remote(
            own.at[a, lines],
            gath.at[a, h, me],
            a_send.at[a, h, k],
            g_recv.at[a, h, me],
            {"chan": plane * GROUP + mate(k)},
        )

    def hop_copy(a, h, s, side):
        return remote(
            gath.at[a, h, s],
            gath.at[a, h, s],
            g_send.at[a, h, side, s],
            g_recv.at[a, h, s],
            {"chan": me + GROUP if side == 0 else me - GROUP},
        )

    to_right, to_left = plane + 1 < planes, plane >= 1

    def pass_on(a, h, s, side):
        @pl.when(to_right if side == 0 else to_left)
        def _():
            hop_copy(a, h, s, side).start()

    def hop_first(a, h, q):
        s = plane * GROUP + mate(q)
        if not (isinstance(q, int) and q == 0):
            hop_copy(a, h, s, 0).wait_recv()
        pass_on(a, h, s, 0)
        pass_on(a, h, s, 1)

    def hop(a, h, t, q):
        @pl.when(plane >= t)
        def _():
            s = (plane - t) * GROUP + mate(q)
            hop_copy(a, h, s, 0).wait_recv()
            pass_on(a, h, s, 0)

        @pl.when(plane + t < planes)
        def _():
            s = (plane + t) * GROUP + mate(q)
            hop_copy(a, h, s, 1).wait_recv()
            pass_on(a, h, s, 1)

    def hops(a, h, t, which=range(GROUP)):
        for q in which:
            hop(a, h, t, q)

    def hops_between(a, h, start, stop):
        @pl.loop(start, stop)
        def _(t):
            hops(a, h, t)

    def scatter(a, h):
        for k in range(1, GROUP):
            spread_copy(a, h, k).start()

    def firsts(a, h, which=range(GROUP)):
        for q in which:
            hop_first(a, h, q)


    scale = jnp.broadcast_to(taps_ref[:, TAPS + 1 : TAPS + 2], (channels, breadth))
    gain = jnp.broadcast_to(taps_ref[:, TAPS : TAPS + 1], (channels, breadth))

    @pl.loop(0, height)
    def _(r):
        padded[r + 3] = image_ref[r].astype(f32)
        own[SCALED, r] = (scale * cotan_ref[r].astype(f32)).astype(bf16)

    gain_src[...] = gain_ref[...]

    def keep_own(a):
        for h in range(CUTS):
            for i in range(pc):
                gath[a, h, me, i] = own[a, lane * part + h * pc + i]

    keep_own(SCALED)
    pl.semaphore_wait(barrier, n + 1 + steps)

    scatter(SCALED, 0)
    firsts(SCALED, 0, [0])

    def edges(index, first, last, arrived):
        return (
            remote(first, arrived.at[1], pair_send.at[index], pair_recv.at[index], {"rows": up}),
            remote(
                last, arrived.at[0], pair_send.at[index + 1], pair_recv.at[index + 1], {"rows": down}
            ),
        )

    def edges_start(upward, downward):
        @pl.when(row > 0)
        def _():
            upward.start()

        @pl.when(row < rows - 1)
        def _():
            downward.start()

    def edges_wait(upward, downward, arrived, target):
        @pl.when(row > 0)
        def _():
            upward.wait_send()
            downward.wait_recv()
            for i in range(3):
                target[i] = arrived[0, i].astype(f32)

        @pl.when(row == 0)
        def _():
            for i in range(3):
                target[i] = jnp.zeros((channels, breadth), f32)

        @pl.when(row < rows - 1)
        def _():
            downward.wait_send()
            upward.wait_recv()
            for i in range(3):
                target[height + 3 + i] = arrived[1, i].astype(f32)

        @pl.when(row == rows - 1)
        def _():
            for i in range(3):
                target[height + 3 + i] = jnp.zeros((channels, breadth), f32)

    image_halos = edges(
        0, image_ref.at[pl.ds(0, 3)], image_ref.at[pl.ds(height - 3, 3)], image_halo
    )
    edges_start(*image_halos)

    def block(a, index):
        return w.at[a, pl.ds(index * hidden, hidden)]

    core_w, far_w = [None] * 2, [None] * 2
    shorter = hidden // 2
    parity = lax.rem(row, 2)

    def near_rows(a):
        return w.at[a, pl.ds(pl.multiple_of(hidden + parity * shorter, 16), shorter)]

    def near_x(a):
        return remote(
            weights_ref.at[a, pl.ds(pl.multiple_of(parity * shorter, 16), shorter)],
            near_rows(a),
            pair_send.at[2 + a],
            pair_recv.at[2 + a],
            {"chan": flipped(me, 2)},
        )

    def near_y(a):
        return remote(
            near_rows(a),
            near_rows(a),
            pair_send.at[10 + a],
            pair_recv.at[10 + a],
            {"rows": partners[0]},
        )

    def near_on(a):
        near_x(a).wait()
        near_y(a).start()

    near_x(1).start()
    near_x(0).start()
    for a in range(2):
        core_w[a] = pair(4 + a, weights_ref.at[a], block(a, 2), {"chan": flipped(me, 1)})

    def gain_copy(k):
        return remote(
            gain_src,
            gain_in.at[me],
            gain_send.at[k],
            gain_recv.at[me],
            {"chan": lax.rem(me + k, n)},
        )

    @pl.loop(1, n)
    def _(k):
        gain_copy(k).start()

    gain_in[me] = gain_ref[...]
    for a in range(2):
        w[a, pl.ds(0, hidden)] = weights_ref[a]

    firsts(SCALED, 0, [1, 2, 3])
    hops(SCALED, 0, 1, [0, 1])
    edges_wait(*image_halos, image_halo, padded)

    def spaced(g, count, first):
        span = groups - first
        low = jnp.maximum(lax.div((g - first) * count, span), 0)
        high = jnp.maximum(lax.div((g + 1 - first) * count, span), 0)
        return jnp.where(g < first, 0, low), jnp.where(g < first, 0, high)

    @pl.loop(0, groups)
    def _(g):
        group = pl.ds(pl.multiple_of(8 * g, 8), 8)
        taps = taps_ref[group, :]
        sums = [None] * height
        for v in range(KSIZE):
            shifts = [shifted(padded[r, group, :], 3 - v) for r in range(height + 6)]
            for u in range(KSIZE):
                t = u * KSIZE + v
                tap = jnp.broadcast_to(taps[:, t : t + 1], taps.shape)
                for r in range(height):
                    term = tap * shifts[r + u]
                    sums[r] = term if sums[r] is None else sums[r] + term
        for r in range(height):
            running[r, group, :] = sums[r]
    @pl.loop(0, height)
    def _(r):
        own[MIXED, r] = running[r].astype(bf16)

    keep_own(MIXED)
    for h in range(CUTS):
        scatter(MIXED, h)
    firsts(MIXED, 0, [0])
    for h in range(1, CUTS):
        scatter(SCALED, h)
    near_on(1)
    hops(SCALED, 0, 1, [2, 3])
    firsts(MIXED, 0, [1])
    hops(SCALED, 0, 2, [0, 1])
    firsts(MIXED, 0, [2, 3])
    hops(SCALED, 0, 2, [2, 3])
    near_on(0)

    @pl.loop(3, planes)
    def _(t):
        hops(SCALED, 0, t)
        hops(MIXED, 0, t - 2)

    firsts(MIXED, 1)
    hops(MIXED, 0, planes - 2)
    firsts(SCALED, 1)
    def far(a):
        near_y(a).wait()
        far_w[a] = pair(6 + a, block(a, 1), block(a, 3), {"chan": flipped(me, 1)})

    far(1)

    def columns(i):
        return pl.ds(pl.multiple_of(i * breadth, breadth), breadth)

    def lay_scaled(h):
        @pl.loop(0, pc)
        def _(i):
            for s in range(0, n, 2):
                both = [gath[SCALED, h, s + k, i].astype(f32) for k in range(2)]
                ns[1, h, pl.ds(s * channels, 2 * channels), columns(i)] = jnp.concatenate(
                    both, axis=0
                ).astype(bf16)

    lay_scaled(0)

    @pl.loop(1, n)
    def _(k):
        copy = remote(
            gain_src,
            gain_in.at[lax.rem(me + n - k, n)],
            gain_send.at[k],
            gain_recv.at[lax.rem(me + n - k, n)],
            {"chan": lax.rem(me + k, n)},
        )
        copy.wait()

    @pl.loop(0, n)
    def _(s):
        square = jnp.broadcast_to(gain_in[s], (breadth, breadth)).T
        gain_cols[s] = square[:channels]

    hops_between(MIXED, 1, 1, planes - 2)
    core_w[1].wait()
    far_w[1].wait()
    double = 2 * hidden

    def half(index):
        return pl.ds(pl.multiple_of(index * double, double), double)

    def back_product(h):
        @pl.loop(0, GROUP // 2)
        def _(index):
            gact[h, half(index)] = jnp.dot(
                w[1, half(index)], ns[1, h], preferred_element_type=f32
            )

    back_product(0)

    def turn(a):
        @pl.loop(0, GROUP * hidden // 128)
        def _(j):
            piece = pl.ds(pl.multiple_of(j * 128, 128), 128)
            wt[a, :, piece] = w[a, piece, :].T

    turn(1)
    far(0)

    def normalized(h):
        @pl.loop(0, pc)
        def _(i):
            total = gath[MIXED, h, 0, i].astype(f32)
            for s in range(1, n):
                total += gath[MIXED, h, s, i].astype(f32)
            centre = jnp.sum(total, axis=0, keepdims=True) * (1.0 / D)
            total = jnp.zeros((channels, breadth), f32)
            for s in range(n):
                total += jnp.square(gath[MIXED, h, s, i].astype(f32) - centre)
            spread = jnp.sum(total, axis=0, keepdims=True) * (1.0 / D)
            inv_scale = lax.rsqrt(spread + epsilon)
            st_out[h * pc + i, 2:3] = centre
            st_out[h * pc + i, 3:4] = inv_scale
            for s in range(0, n, 2):
                both = [
                    (gath[MIXED, h, s + k, i].astype(f32) - centre) * inv_scale * gain_cols[s + k]
                    for k in range(2)
                ]
                ns[0, h, pl.ds(s * channels, 2 * channels), columns(i)] = jnp.concatenate(
                    both, axis=0
                ).astype(bf16)

    def product(h):
        @pl.loop(0, GROUP // 2)
        def _(index):
            pre[half(index)] = jnp.dot(w[0, half(index)], ns[0, h], preferred_element_type=f32)

    def activate(h):
        @pl.loop(0, GROUP * hidden // 32)
        def _(j):
            lines = pl.ds(pl.multiple_of(j * 32, 32), 32)
            value = pre[lines]
            cdf = 0.5 * (1.0 + lax.erf(value * inv_root_two))
            slope = cdf + value * jnp.exp(-0.5 * value * value) * inv_root_two_pi
            ag[1, h, lines] = (value * cdf).astype(bf16)
            ag[0, h, lines] = (gact[h, lines] * slope).astype(bf16)

    def sum_copy(a, h, p, side):
        target = p if side == 0 else jnp.where(p == plane - 1, planes, p)
        return remote(
            red_out.at[a, h, p],
            red_in.at[a, h, target],
            r_send.at[a, h, p],
            r_recv.at[a, h, target],
            {"chan": me + GROUP if side == 0 else me - GROUP},
        )

    def round_out(a, h, p):
        @pl.loop(0, GROUP)
        def _(q):
            for i in range(pc):
                red_out[a, h, p, q, i] = part_sum[a, h, p, q, i].astype(bf16)

    def take(a, h, p, index):
        copy = remote(
            red_out.at[a, h, p],
            red_in.at[a, h, index],
            r_send.at[a, h, p],
            r_recv.at[a, h, index],
            {"chan": lax.rem(me + GROUP, n)},
        )
        copy.wait_recv()

        @pl.loop(0, GROUP)
        def _(q):
            for i in range(pc):
                part_sum[a, h, p, q, i] += red_in[a, h, index, q, i].astype(f32)

    def partial(a, h):
        @pl.loop(0, planes)
        def _(p):
            lines = pl.ds(pl.multiple_of(p * band, band), band)
            result = jnp.dot(wt[a, lines], ag[a, h], preferred_element_type=f32)
            for q in range(GROUP):
                for i in range(pc):
                    part_sum[a, h, p, q, i] = result[
                        q * channels : (q + 1) * channels, i * breadth : (i + 1) * breadth
                    ]

    def emit(a, h):
        @pl.loop(0, planes - 1)
        def _(j):
            @pl.when(plane == 0)
            def _():
                round_out(a, h, planes - 1 - j)
                sum_copy(a, h, planes - 1 - j, 0).start()

            @pl.when(plane == planes - 1)
            def _():
                round_out(a, h, j)
                sum_copy(a, h, j, 1).start()

    def relay(a, h, tau):
        right = planes - 1 - tau + plane

        @pl.when((plane > 0) & (right < planes))
        def _():
            take(a, h, right, right)
            round_out(a, h, right)
            sum_copy(a, h, right, 0).start()

        left = tau - (planes - 1 - plane)

        @pl.when((plane < planes - 1) & (left >= 0))
        def _():
            take(a, h, left, left)
            round_out(a, h, left)
            sum_copy(a, h, left, 1).start()

    def piece_copy(a, h, k):
        return remote(
            red_out.at[a, h, plane, mate(k)],
            piece_in.at[a, pl.ds(lane * part + h * pc, pc)],
            p_send.at[a, h, k],
            p_recv.at[a, h, lane],
            {"chan": plane * GROUP + mate(k)},
        )

    def finals(a, h):
        @pl.when(plane > 0)
        def _():
            take(a, h, plane, plane)

        @pl.when(plane < planes - 1)
        def _():
            take(a, h, plane, planes)

        round_out(a, h, plane)
        for k in range(1, GROUP):
            piece_copy(a, h, k).start()
        for i in range(pc):
            piece_in[a, lane * part + h * pc + i] = red_out[a, h, plane, lane, i]

    def pieces(a, h):
        for k in range(1, GROUP):
            source = mate(k)
            copy = remote(
                red_out.at[a, h, plane, mate(k)],
                piece_in.at[a, pl.ds(source * part + h * pc, pc)],
                p_send.at[a, h, k],
                p_recv.at[a, h, source],
                {"chan": plane * GROUP + mate(k)},
            )
            copy.wait()

    def stats_copy(h, k):
        other = lax.rem(plane + k, planes)
        return remote(
            st_out.at[pl.ds(h * pc, pc)],
            st_in.at[plane, pl.ds(h * pc, pc)],
            s_send.at[h, k],
            s_recv.at[h, plane],
            {"chan": other * GROUP + lane},
        )

    def stats(h):
        @pl.loop(0, pc)
        def _(i):
            centre, inv_scale = st_out[h * pc + i, 2:3], st_out[h * pc + i, 3:4]
            one = jnp.zeros((channels, breadth), f32)
            two = jnp.zeros((channels, breadth), f32)
            for s in range(n):
                gained = part_sum[NORMED, h, s // GROUP, s % GROUP, i] * gain_cols[s]
                one += gained
                two += gained * ((gath[MIXED, h, s, i].astype(f32) - centre) * inv_scale)
            st_out[h * pc + i, 0:1] = jnp.sum(one, axis=0, keepdims=True)
            st_out[h * pc + i, 1:2] = jnp.sum(two, axis=0, keepdims=True)

        for k in range(1, planes):
            stats_copy(h, k).start()

    def stats_total(h):
        for k in range(1, planes):
            source = lax.rem(plane + planes - k, planes)
            copy = remote(
                st_out.at[pl.ds(h * pc, pc)],
                st_in.at[source, pl.ds(h * pc, pc)],
                s_send.at[h, k],
                s_recv.at[h, source],
                {"chan": lax.rem(plane + k, planes) * GROUP + lane},
            )
            copy.wait()
        for i in range(pc):
            here = h * pc + i
            total = st_out[here]
            for k in range(1, planes):
                total += st_in[lax.rem(plane + k, planes), here]
            line = lane * part + here
            st_all[line, 0:2] = total[0:2]
            st_all[line, 2:4] = st_out[here, 2:4]
        for k in range(1, GROUP):
            lines = pl.ds(lane * part + h * pc, pc)
            remote(
                st_all.at[lines],
                st_all.at[lines],
                t_send.at[h, k],
                t_recv.at[h, lane],
                {"chan": plane * GROUP + mate(k)},
            ).start()

    def stats_pieces(h):
        for k in range(1, GROUP):
            source = mate(k)
            copy = remote(
                st_all.at[pl.ds(lane * part + h * pc, pc)],
                st_all.at[pl.ds(source * part + h * pc, pc)],
                t_send.at[h, k],
                t_recv.at[h, source],
                {"chan": plane * GROUP + mate(k)},
            )
            copy.wait()

    contract_tail = (((1,), (1,)), ((), ()))

    def weight_grad(a, index):
        lines = pl.ds(index * hidden, hidden)
        total = lax.dot_general(
            ag[a, 0, lines], ns[a, 0], contract_tail, preferred_element_type=f32
        )
        for h in range(1, CUTS):
            total += lax.dot_general(
                ag[a, h, lines], ns[a, h], contract_tail, preferred_element_type=f32
            )
        return total

    def relays(a, h, start, stop):
        @pl.loop(start, stop)
        def _(tau):
            relay(a, h, tau)

    hops(MIXED, 0, planes - 1)
    normalized(0)
    core_w[0].wait()
    far_w[0].wait()
    turn(0)
    product(0)
    activate(0)
    hops(MIXED, 1, planes - 2)
    hops_between(SCALED, 1, 1, planes - 2)
    partial(NORMED, 0)
    stats(0)
    emit(NORMED, 0)
    partial(BRANCH, 0)
    emit(BRANCH, 0)
    hops(MIXED, 1, planes - 1)
    normalized(1)
    product(1)
    hops(SCALED, 1, planes - 2)
    relay(NORMED, 0, 1)
    hops(SCALED, 1, planes - 1)
    lay_scaled(1)
    back_product(1)
    activate(1)
    partial(NORMED, 1)
    stats(1)
    emit(NORMED, 1)

    def halves(c):
        return c // 2, pl.ds(c % 2 * shorter, shorter)

    def near_grad(c):
        a, lines = halves(c)
        return remote(
            near_out.at[a, lines],
            near_in.at[a, lines],
            pair_send.at[14 + c],
            pair_recv.at[14 + c],
            {"chan": flipped(me, 2)},
        )

    def row_step(c, s):
        a, lines = halves(c)
        index = 18 + 4 * s + c
        return remote(
            row_out.at[s, a, lines],
            row_in.at[s, a, lines],
            pair_send.at[index],
            pair_recv.at[index],
            {"rows": partners[s]},
        )

    def row_begin(c):
        near_grad(c).wait()
        a, first = c // 2, c % 2 * (shorter // 16)

        @pl.loop(first, first + shorter // 16)
        def _(i):
            mine = pl.ds(pl.multiple_of(16 * i, 16), 16)
            row_out[0, a, mine, :] = (
                grads_ref[a, mine, :] + near_in[a, mine, :].astype(f32)
            ).astype(bf16)

        row_step(c, 0).start()

    relays(NORMED, 0, 2, planes - 1)
    core = [None] * 2
    for a in range(2):
        for index in range(2):
            sent[a, pl.ds(index * hidden, hidden)] = weight_grad(a, 2 + index).astype(bf16)
        core[a] = pair(8 + a, sent.at[a], core_in.at[a], {"chan": flipped(me, 1)})
    relay(BRANCH, 0, 1)
    for a in range(2):
        for index in range(2):
            kept[a, pl.ds(index * hidden, hidden)] = weight_grad(a, index)
    finals(NORMED, 0)
    for a in range(2):
        core[a].wait()

        @pl.loop(0, hidden // 16)
        def _(i):
            mine = pl.ds(pl.multiple_of(16 * i, 16), 16)
            other = pl.ds(pl.multiple_of(hidden + 16 * i, 16), 16)
            grads_ref[a, mine, :] = kept[a, mine, :] + core_in[a, mine, :].astype(f32)
            near_out[a, mine, :] = (kept[a, other, :] + core_in[a, other, :].astype(f32)).astype(
                bf16
            )

        if a == 0:
            near_grad(0).start()
            near_grad(1).start()

    relays(BRANCH, 0, 2, planes - 1)
    partial(BRANCH, 1)
    emit(BRANCH, 1)
    relay(NORMED, 1, 1)
    for a in range(2):
        for h in range(CUTS):
            for k in range(1, GROUP):
                spread_copy(a, h, k).wait_send()

            @pl.loop(0, n)
            def _(s):
                home = lax.div(s, GROUP)

                @pl.when(to_right & (home <= plane))
                def _():
                    hop_copy(a, h, s, 0).wait_send()

                @pl.when(to_left & (home >= plane))
                def _():
                    hop_copy(a, h, s, 1).wait_send()

    stats_total(0)
    near_grad(2).start()
    finals(BRANCH, 0)
    relays(NORMED, 1, 2, planes - 1)
    for h in range(1, CUTS):
        stats_total(h)
    row_begin(0)
    finals(NORMED, 1)
    near_grad(3).start()
    row_begin(1)
    for h in range(CUTS):
        stats_pieces(h)
        pieces(NORMED, h)

    sums_one[...] = jnp.zeros_like(sums_one)
    sums_two[...] = jnp.zeros_like(sums_two)

    def normalize(start, stop):
        @pl.loop(start, stop)
        def _(r):
            grad_normed = piece_in[NORMED, r].astype(f32)
            line = st_all[r]
            centre, inv_scale = line[2:3], line[3:4]
            unit = (own[MIXED, r].astype(f32) - centre) * inv_scale
            sums_one[...] += grad_normed * unit
            scaled_grad = grad_normed * gain
            mixed_grad = inv_scale * (
                scaled_grad - line[0:1] * (1.0 / D) - unit * (line[1:2] * (1.0 / D))
            )
            grad_pad[r + 3] = mixed_grad.astype(bf16).astype(f32)

    normalize(0, 3)
    normalize(height - 3, height)
    for i in range(3):
        halo_out[0, i] = grad_pad[3 + i].astype(bf16)
        halo_out[1, i] = grad_pad[height + i].astype(bf16)
    halos = edges(12, halo_out.at[0], halo_out.at[1], halo_in)
    edges_start(*halos)
    normalize(3, height - 3)
    row_begin(2)
    events = planes - 2

    @pl.loop(0, groups)
    def _(g):
        group = pl.ds(pl.multiple_of(8 * g, 8), 8)
        for v in range(KSIZE):
            shifts = [shifted(grad_pad[r + 3, group, :], v - 3) for r in range(height)]
            for u in range(KSIZE):
                both = [shifts[r] * padded[r + u, group, :] for r in range(height)]
                while len(both) > 1:
                    both = [p + q for p, q in zip(both[::2], both[1::2])] + both[
                        len(both) // 2 * 2 :
                    ]
                products[u * KSIZE + v, group, :] = both[0]
        low, high = spaced(g, events, 0)

        @pl.loop(low, high)
        def _(e):
            relay(BRANCH, 1, 1 + e)

        @pl.when(g == groups // 2)
        def _():
            row_begin(3)

    lane_sum = jnp.dot(
        products[...].reshape(TAPS * channels, breadth),
        jnp.ones((breadth, 128), f32),
        precision=lax.Precision.HIGHEST,
        preferred_element_type=f32,
    ).reshape(TAPS, channels, 128)
    position = lax.broadcasted_iota(jnp.int32, small_ref.shape, 1)
    taps_grad = jnp.zeros(small_ref.shape, f32)
    for t in range(TAPS):
        taps_grad = jnp.where(position == t, lane_sum[t], taps_grad)
    small_ref[...] = jnp.where(
        position == TAPS, jnp.sum(sums_one[...], axis=1, keepdims=True), taps_grad
    )

    def exchange(chain, s, value):
        small_out[chain, s] = value
        return pair(
            18 + 4 * steps + chain * steps + s,
            small_out.at[chain, s],
            small_in.at[chain, s],
            {"rows": partners[s]},
        )

    step = exchange(0, 0, small_ref[...])
    finals(BRANCH, 1)
    edges_wait(*halos, halo_in, grad_pad)

    @pl.loop(0, groups)
    def _(g):
        group = pl.ds(pl.multiple_of(8 * g, 8), 8)
        taps = taps_ref[group, :]
        sums = [None] * height
        for v in range(KSIZE):
            shifts = [shifted(grad_pad[r, group, :], v - 3) for r in range(height + 6)]
            for u in range(KSIZE):
                t = u * KSIZE + v
                tap = jnp.broadcast_to(taps[:, t : t + 1], taps.shape)
                for r in range(height):
                    term = tap * shifts[r + 6 - u]
                    sums[r] = term if sums[r] is None else sums[r] + term
        for r in range(height):
            running[r, group, :] = sums[r]

    @pl.loop(0, height)
    def _(r):
        image_grad_ref[r] = (running[r] + cotan_ref[r].astype(f32)).astype(bf16)

    for s in range(steps):
        for c in range(4):
            row_step(c, s).wait()
            final = s == steps - 1
            a, first = c // 2, c % 2 * (shorter // 16)

            @pl.loop(first, first + shorter // 16)
            def _(i):
                mine = pl.ds(pl.multiple_of(16 * i, 16), 16)
                total = row_out[s, a, mine, :].astype(f32) + row_in[s, a, mine, :].astype(f32)
                if final:
                    grads_ref[a, mine, :] = total
                else:
                    row_out[s + 1, a, mine, :] = total.astype(bf16)

            if not final:
                row_step(c, s + 1).start()

    for h in range(CUTS):
        pieces(BRANCH, h)

    @pl.loop(0, height)
    def _(r):
        branch = piece_in[BRANCH, r].astype(f32)
        sums_two[...] += branch * cotan_ref[r].astype(f32)
        block_ref[r] = (image_ref[r].astype(f32) + scale * branch).astype(bf16)

    total = jnp.broadcast_to(jnp.sum(sums_two[...], axis=1, keepdims=True), small_ref.shape)
    last = exchange(1, 0, total)
    small = small_ref[...]
    for s in range(steps):
        step.wait()
        small = small + small_in[0, s]
        if s + 1 < steps:
            step = exchange(0, s + 1, small)
    for s in range(steps):
        last.wait()
        total = total + small_in[1, s]
        if s + 1 < steps:
            last = exchange(1, s + 1, total)
    small_ref[...] = jnp.where(position == TAPS + 1, total, small)

    for a in range(2):
        for h in range(CUTS):

            @pl.loop(0, planes)
            def _(p):
                @pl.when(p > plane)
                def _():
                    sum_copy(a, h, p, 0).wait_send()

                @pl.when(p < plane)
                def _():
                    sum_copy(a, h, p, 1).wait_send()


def run_block(n, arrays):
    f32, bf16 = jnp.float32, jnp.bfloat16
    height, channels, breadth = arrays[0].shape
    hidden, width = arrays[4].shape[1:]
    planes = n // GROUP
    part = height // GROUP
    pc = part // CUTS
    every = GROUP * hidden
    pixels = pc * breadth
    rows = lax.axis_size("rows")
    steps = rows.bit_length() - 1
    pairs = 18 + 6 * steps
    vmem = pl.BlockSpec(memory_space=pltpu.VMEM)
    dma = pltpu.SemaphoreType.DMA
    return pl.pallas_call(
        functools.partial(block_kernel, n, rows),
        out_shape=(
            jax.ShapeDtypeStruct((height, channels, breadth), bf16),
            jax.ShapeDtypeStruct((height, channels, breadth), bf16),
            jax.ShapeDtypeStruct((channels, 128), f32),
            jax.ShapeDtypeStruct((2, hidden, width), f32),
        ),
        in_specs=[vmem] * 5,
        out_specs=(vmem, vmem, vmem, vmem),
        scratch_shapes=[
            pltpu.VMEM((height + 6, channels, breadth), f32),
            pltpu.VMEM((height, channels, breadth), f32),
            pltpu.VMEM((2, height, channels, breadth), bf16),
            pltpu.VMEM((2, CUTS, n, pc, channels, breadth), bf16),
            pltpu.VMEM((1, 128), f32),
            pltpu.VMEM((n, 1, 128), f32),
            pltpu.VMEM((n, channels, breadth), f32),
            pltpu.VMEM((2, every, width), bf16),
            pltpu.VMEM((2, width, every), bf16),
            pltpu.VMEM((2, CUTS, width, pixels), bf16),
            pltpu.VMEM((CUTS, every, pixels), f32),
            pltpu.VMEM((every, pixels), f32),
            pltpu.VMEM((2, CUTS, every, pixels), bf16),
            pltpu.VMEM((2, CUTS, planes, GROUP, pc, channels, breadth), f32),
            pltpu.VMEM((2, CUTS, planes, GROUP, pc, channels, breadth), bf16),
            pltpu.VMEM((2, CUTS, planes + 1, GROUP, pc, channels, breadth), bf16),
            pltpu.VMEM((2, height, channels, breadth), bf16),
            pltpu.VMEM((part, 4, breadth), f32),
            pltpu.VMEM((planes, part, 4, breadth), f32),
            pltpu.VMEM((height, 4, breadth), f32),
            pltpu.VMEM((2, 2 * hidden, width), f32),
            pltpu.VMEM((2, 2 * hidden, width), bf16),
            pltpu.VMEM((2, 2 * hidden, width), bf16),
            pltpu.VMEM((2, hidden, width), bf16),
            pltpu.VMEM((2, hidden, width), bf16),
            pltpu.VMEM((steps, 2, hidden, width), bf16),
            pltpu.VMEM((steps, 2, hidden, width), bf16),
            pltpu.VMEM((height + 6, channels, breadth), f32),
            pltpu.VMEM((channels, breadth), f32),
            pltpu.VMEM((channels, breadth), f32),
            pltpu.VMEM((TAPS, channels, breadth), f32),
            pltpu.VMEM((2, 3, channels, breadth), bf16),
            pltpu.VMEM((2, 3, channels, breadth), bf16),
            pltpu.VMEM((2, 3, channels, breadth), bf16),
            pltpu.VMEM((2, steps, channels, 128), f32),
            pltpu.VMEM((2, steps, channels, 128), f32),
            dma((2, CUTS, GROUP)),
            dma((2, CUTS, 2, n)),
            dma((2, CUTS, n)),
            dma((n,)),
            dma((n,)),
            dma((2, CUTS, planes)),
            dma((2, CUTS, planes + 1)),
            dma((2, CUTS, GROUP)),
            dma((2, CUTS, GROUP)),
            dma((CUTS, planes)),
            dma((CUTS, planes)),
            dma((CUTS, GROUP)),
            dma((CUTS, GROUP)),
            dma((pairs,)),
            dma((pairs,)),
        ],
        compiler_params=pltpu.CompilerParams(
            collective_id=0, has_side_effects=True, vmem_limit_bytes=52 * 2**20
        ),
        cost_estimate=pl.CostEstimate(
            flops=4000000000, bytes_accessed=10000000, transcendentals=0
        ),
    )(*arrays)


def body(image, dw_kernel, ln_gain, w_in, w_out, layer_scale, cotangent):
    channels = image.shape[0]
    n = lax.axis_size("chan")
    image_rows = jnp.transpose(image[:, 0], (1, 0, 2))
    cotan_rows = jnp.transpose(cotangent[:, 0], (1, 0, 2))
    taps = jnp.concatenate(
        [
            dw_kernel.reshape(channels, TAPS),
            ln_gain[:, None],
            layer_scale[:, None],
            jnp.zeros((channels, 128 - TAPS - 2), jnp.float32),
        ],
        axis=1,
    )
    gain_row = jnp.pad(ln_gain[None, :], ((0, 0), (0, 128 - channels)))
    block_out, image_grad, small, grads = run_block(
        n, (image_rows, cotan_rows, taps, gain_row, jnp.stack([w_in.T, w_out]))
    )
    return (
        jnp.transpose(block_out, (1, 0, 2))[:, None],
        jnp.transpose(image_grad, (1, 0, 2))[:, None],
        small[:, :TAPS].reshape(channels, KSIZE, KSIZE),
        small[:, TAPS],
        small[:, TAPS + 1],
        grads[0].T,
        grads[1],
    )


def solution(mesh):
    return jax.shard_map(
        body,
        mesh=mesh,
        in_specs=(
            P("chan", None, "rows", None),
            P("chan", None, None),
            P("chan"),
            P(None, "chan"),
            P("chan", None),
            P("chan"),
            P("chan", None, "rows", None),
        ),
        out_specs=(
            P("chan", None, "rows", None),
            P("chan", None, "rows", None),
            P("chan", None, None),
            P("chan"),
            P("chan"),
            P(None, "chan"),
            P("chan", None),
        ),
        check_vma=False,
    )
```

```python
import functools

import jax
import jax.numpy as jnp
from jax import lax
from jax.experimental import pallas as pl
from jax.experimental.pallas import tpu as pltpu
from jax.sharding import PartitionSpec as P

D = 768
KSIZE = 7
PITCH = 8
TAPS = KSIZE * PITCH


epsilon = 1e-06
inv_root_two = 0.7071067811865476
inv_root_two_pi = 0.3989422804014327

GROUP = 4
CUTS = 2
MESH = pl.DeviceIdType.MESH
MIXED, SCALED = 0, 1
NORMED, BRANCH = 0, 1


def shifted(value, shift):
    if shift == 0:
        return value
    breadth = value.shape[1]
    lane = lax.broadcasted_iota(jnp.int32, value.shape, 1)
    rolled = pltpu.roll(value, shift % breadth, 1)
    keep = lane >= shift if shift > 0 else lane < breadth + shift
    return jnp.where(keep, rolled, 0.0)


def flipped(index, bit):
    return index + bit - 2 * bit * lax.rem(lax.div(index, bit), 2)


def block_kernel(
    n,
    rows,
    image_hbm,
    cotan_hbm,
    kernel_hbm,
    gain_hbm,
    scale_hbm,
    w_in_ref,
    w_out_ref,
    block_ref,
    image_grad_ref,
    packed_ref,
    grad_in_ref,
    grad_out_ref,
    image_ref,
    cotan_ref,
    kernel_ref,
    gain_ref,
    scale_ref,
    square,
    taps_ref,
    small_ref,
    cotan,
    image_edge,
    padded,
    running,
    own,
    gath,
    gain_src,
    gain_in,
    gain_cols,
    w,
    wt,
    ns,
    gact,
    pre,
    ag,
    part_sum,
    red_out,
    red_in,
    piece_in,
    st_out,
    st_in,
    st_all,
    kept,
    sent,
    core_in,
    near_out,
    near_in,
    row_out,
    row_in,
    grad_pad,
    sums_one,
    sums_two,
    products,
    image_halo,
    halo_out,
    halo_in,
    small_out,
    small_in,
    in_sem,
    a_send,
    g_send,
    g_recv,
    gain_send,
    gain_recv,
    r_send,
    r_recv,
    p_send,
    p_recv,
    s_send,
    s_recv,
    t_send,
    t_recv,
    pair_send,
    pair_recv,
):
    f32, bf16 = jnp.float32, jnp.bfloat16
    me = lax.axis_index("chan")
    row = lax.axis_index("rows")
    plane, lane = lax.div(me, GROUP), lax.rem(me, GROUP)
    channels, height, breadth = image_ref.shape
    weights, grads_ref = (w_in_ref, w_out_ref), (grad_in_ref, grad_out_ref)
    planes = n // GROUP
    part = height // GROUP
    pc = part // CUTS
    hidden = w_in_ref.shape[0]
    width = w_in_ref.shape[1]
    band = GROUP * channels
    steps = row_out.shape[0]
    groups = channels // 8
    up, down = lax.rem(row + rows - 1, rows), lax.rem(row + 1, rows)
    partners = [flipped(row, 2**s) for s in range(steps)]

    barrier = pltpu.get_barrier_semaphore()
    for k in range(1, n):
        pl.semaphore_signal(
            barrier, inc=1, device_id={"chan": lax.rem(me + k, n)}, device_id_type=MESH
        )
    for other in [up, down] + partners:
        pl.semaphore_signal(barrier, inc=1, device_id={"rows": other}, device_id_type=MESH)

    fetched = [
        (image_hbm, image_ref),
        (cotan_hbm, cotan_ref),
        (kernel_hbm, kernel_ref),
        (gain_hbm, gain_ref),
        (scale_hbm, scale_ref),
        (w_in_ref, w.at[0, pl.ds(0, hidden)]),
        (w_out_ref, w.at[1, pl.ds(0, hidden)]),
    ]
    fetches = [
        pltpu.make_async_copy(source, target, in_sem.at[i])
        for i, (source, target) in enumerate(fetched)
    ]
    for copy in fetches:
        copy.start()

    def remote(source, target, send, recv, device):
        return pltpu.make_async_remote_copy(
            src_ref=source,
            dst_ref=target,
            send_sem=send,
            recv_sem=recv,
            device_id=device,
            device_id_type=MESH,
        )

    def pair(index, source, target, device):
        copy = remote(source, target, pair_send.at[index], pair_recv.at[index], device)
        copy.start()
        return copy

    def mate(k):
        return flipped(flipped(lane, 1), 2) if k == 3 else flipped(lane, k) if k else lane


    def spread_copy(a, h, k):
        lines = pl.ds(mate(k) * part + h * pc, pc)
        return remote(
            own.at[a, lines],
            gath.at[a, h, me],
            a_send.at[a, h, k],
            g_recv.at[a, h, me],
            {"chan": plane * GROUP + mate(k)},
        )

    def hop_copy(a, h, s, side):
        return remote(
            gath.at[a, h, s],
            gath.at[a, h, s],
            g_send.at[a, h, side, s],
            g_recv.at[a, h, s],
            {"chan": me + GROUP if side == 0 else me - GROUP},
        )

    to_right, to_left = plane + 1 < planes, plane >= 1

    def pass_on(a, h, s, side):
        @pl.when(to_right if side == 0 else to_left)
        def _():
            hop_copy(a, h, s, side).start()

    def hop_first(a, h, q):
        s = plane * GROUP + mate(q)
        if not (isinstance(q, int) and q == 0):
            hop_copy(a, h, s, 0).wait_recv()
        pass_on(a, h, s, 0)
        pass_on(a, h, s, 1)

    def hop(a, h, t, q):
        @pl.when(plane >= t)
        def _():
            s = (plane - t) * GROUP + mate(q)
            hop_copy(a, h, s, 0).wait_recv()
            pass_on(a, h, s, 0)

        @pl.when(plane + t < planes)
        def _():
            s = (plane + t) * GROUP + mate(q)
            hop_copy(a, h, s, 1).wait_recv()
            pass_on(a, h, s, 1)

    def hops(a, h, t, which=range(GROUP)):
        for q in which:
            hop(a, h, t, q)

    def hops_between(a, h, start, stop):
        @pl.loop(start, stop)
        def _(t):
            hops(a, h, t)

    def scatter(a, h):
        for k in range(1, GROUP):
            spread_copy(a, h, k).start()

    def firsts(a, h, which=range(GROUP)):
        for q in which:
            hop_first(a, h, q)


    for copy in fetches[2:5]:
        copy.wait()
    square[...] = jnp.zeros_like(square)
    for u in range(KSIZE):
        square[u * PITCH : u * PITCH + KSIZE, 0:channels] = kernel_ref[u]
    square[TAPS : TAPS + 1, 0:channels] = gain_ref[...]
    square[TAPS + 1 : TAPS + 2, 0:channels] = scale_ref[...]
    gain_src[...] = square[TAPS : TAPS + 1]
    taps_ref[...] = square[...].T[:channels]
    scale = jnp.broadcast_to(taps_ref[:, TAPS + 1 : TAPS + 2], (channels, breadth))
    gain = jnp.broadcast_to(taps_ref[:, TAPS : TAPS + 1], (channels, breadth))

    for copy in fetches[:2]:
        copy.wait()

    @pl.loop(0, groups)
    def _(g):
        group = pl.ds(pl.multiple_of(8 * g, 8), 8)
        padded[pl.ds(3, height), group, :] = jnp.swapaxes(image_ref[group].astype(f32), 0, 1)
        cotan[:, group, :] = jnp.swapaxes(cotan_ref[group].astype(f32), 0, 1)

    @pl.loop(0, height)
    def _(r):
        own[SCALED, r] = (scale * cotan[r]).astype(bf16)

    for i in range(3):
        image_edge[0, i] = padded[3 + i].astype(bf16)
        image_edge[1, i] = padded[height + i].astype(bf16)

    def keep_own(a):
        for h in range(CUTS):
            for i in range(pc):
                gath[a, h, me, i] = own[a, lane * part + h * pc + i]

    keep_own(SCALED)
    pl.semaphore_wait(barrier, n + 1 + steps)

    scatter(SCALED, 0)
    firsts(SCALED, 0, [0])

    def edges(index, first, last, arrived):
        return (
            remote(first, arrived.at[1], pair_send.at[index], pair_recv.at[index], {"rows": up}),
            remote(
                last, arrived.at[0], pair_send.at[index + 1], pair_recv.at[index + 1], {"rows": down}
            ),
        )

    def edges_start(upward, downward):
        @pl.when(row > 0)
        def _():
            upward.start()

        @pl.when(row < rows - 1)
        def _():
            downward.start()

    def edges_wait(upward, downward, arrived, target):
        @pl.when(row > 0)
        def _():
            upward.wait_send()
            downward.wait_recv()
            for i in range(3):
                target[i] = arrived[0, i].astype(f32)

        @pl.when(row == 0)
        def _():
            for i in range(3):
                target[i] = jnp.zeros((channels, breadth), f32)

        @pl.when(row < rows - 1)
        def _():
            downward.wait_send()
            upward.wait_recv()
            for i in range(3):
                target[height + 3 + i] = arrived[1, i].astype(f32)

        @pl.when(row == rows - 1)
        def _():
            for i in range(3):
                target[height + 3 + i] = jnp.zeros((channels, breadth), f32)

    image_halos = edges(
        0, image_edge.at[0], image_edge.at[1], image_halo
    )
    edges_start(*image_halos)

    def block(a, index):
        return w.at[a, pl.ds(index * hidden, hidden)]

    core_w, far_w = [None] * 2, [None] * 2
    shorter = hidden // 2
    parity = lax.rem(row, 2)

    def near_rows(a):
        return w.at[a, pl.ds(pl.multiple_of(hidden + parity * shorter, 16), shorter)]

    def near_x(a):
        return remote(
            weights[a].at[pl.ds(pl.multiple_of(parity * shorter, 16), shorter)],
            near_rows(a),
            pair_send.at[2 + a],
            pair_recv.at[2 + a],
            {"chan": flipped(me, 2)},
        )

    def near_y(a):
        return remote(
            near_rows(a),
            near_rows(a),
            pair_send.at[10 + a],
            pair_recv.at[10 + a],
            {"rows": partners[0]},
        )

    def near_on(a):
        near_x(a).wait()
        near_y(a).start()

    near_x(1).start()
    near_x(0).start()
    for a in range(2):
        core_w[a] = pair(4 + a, weights[a], block(a, 2), {"chan": flipped(me, 1)})

    def gain_copy(k):
        return remote(
            gain_src,
            gain_in.at[me],
            gain_send.at[k],
            gain_recv.at[me],
            {"chan": lax.rem(me + k, n)},
        )

    @pl.loop(1, n)
    def _(k):
        gain_copy(k).start()

    gain_in[me] = gain_src[...]
    for copy in fetches[5:]:
        copy.wait()

    firsts(SCALED, 0, [1, 2, 3])
    hops(SCALED, 0, 1, [0, 1])
    edges_wait(*image_halos, image_halo, padded)

    def spaced(g, count, first):
        span = groups - first
        low = jnp.maximum(lax.div((g - first) * count, span), 0)
        high = jnp.maximum(lax.div((g + 1 - first) * count, span), 0)
        return jnp.where(g < first, 0, low), jnp.where(g < first, 0, high)

    @pl.loop(0, groups)
    def _(g):
        group = pl.ds(pl.multiple_of(8 * g, 8), 8)
        taps = taps_ref[group, :]
        sums = [None] * height
        for v in range(KSIZE):
            shifts = [shifted(padded[r, group, :], 3 - v) for r in range(height + 6)]
            for u in range(KSIZE):
                t = u * PITCH + v
                tap = jnp.broadcast_to(taps[:, t : t + 1], taps.shape)
                for r in range(height):
                    term = tap * shifts[r + u]
                    sums[r] = term if sums[r] is None else sums[r] + term
        for r in range(height):
            running[r, group, :] = sums[r]
    @pl.loop(0, height)
    def _(r):
        own[MIXED, r] = running[r].astype(bf16)

    keep_own(MIXED)
    for h in range(CUTS):
        scatter(MIXED, h)
    firsts(MIXED, 0, [0])
    for h in range(1, CUTS):
        scatter(SCALED, h)
    near_on(1)
    hops(SCALED, 0, 1, [2, 3])
    firsts(MIXED, 0, [1])
    hops(SCALED, 0, 2, [0, 1])
    firsts(MIXED, 0, [2, 3])
    hops(SCALED, 0, 2, [2, 3])
    near_on(0)

    @pl.loop(3, planes)
    def _(t):
        hops(SCALED, 0, t)
        hops(MIXED, 0, t - 2)

    firsts(MIXED, 1)
    hops(MIXED, 0, planes - 2)
    firsts(SCALED, 1)
    def far(a):
        near_y(a).wait()
        far_w[a] = pair(6 + a, block(a, 1), block(a, 3), {"chan": flipped(me, 1)})

    far(1)

    def columns(i):
        return pl.ds(pl.multiple_of(i * breadth, breadth), breadth)

    def lay_scaled(h):
        @pl.loop(0, pc)
        def _(i):
            for s in range(0, n, 2):
                both = [gath[SCALED, h, s + k, i].astype(f32) for k in range(2)]
                ns[1, h, pl.ds(s * channels, 2 * channels), columns(i)] = jnp.concatenate(
                    both, axis=0
                ).astype(bf16)

    lay_scaled(0)

    @pl.loop(1, n)
    def _(k):
        copy = remote(
            gain_src,
            gain_in.at[lax.rem(me + n - k, n)],
            gain_send.at[k],
            gain_recv.at[lax.rem(me + n - k, n)],
            {"chan": lax.rem(me + k, n)},
        )
        copy.wait()

    @pl.loop(0, n)
    def _(s):
        square = jnp.broadcast_to(gain_in[s], (breadth, breadth)).T
        gain_cols[s] = square[:channels]

    hops_between(MIXED, 1, 1, planes - 2)
    core_w[1].wait()
    far_w[1].wait()
    double = 2 * hidden

    def half(index):
        return pl.ds(pl.multiple_of(index * double, double), double)

    def back_product(h):
        @pl.loop(0, GROUP // 2)
        def _(index):
            gact[h, half(index)] = jnp.dot(
                w[1, half(index)], ns[1, h], preferred_element_type=f32
            )

    back_product(0)

    def turn(a):
        @pl.loop(0, GROUP * hidden // 128)
        def _(j):
            piece = pl.ds(pl.multiple_of(j * 128, 128), 128)
            wt[a, :, piece] = w[a, piece, :].T

    turn(1)
    far(0)

    def normalized(h):
        @pl.loop(0, pc)
        def _(i):
            total = gath[MIXED, h, 0, i].astype(f32)
            for s in range(1, n):
                total += gath[MIXED, h, s, i].astype(f32)
            centre = jnp.sum(total, axis=0, keepdims=True) * (1.0 / D)
            total = jnp.zeros((channels, breadth), f32)
            for s in range(n):
                total += jnp.square(gath[MIXED, h, s, i].astype(f32) - centre)
            spread = jnp.sum(total, axis=0, keepdims=True) * (1.0 / D)
            inv_scale = lax.rsqrt(spread + epsilon)
            st_out[h * pc + i, 2:3] = centre
            st_out[h * pc + i, 3:4] = inv_scale
            for s in range(0, n, 2):
                both = [
                    (gath[MIXED, h, s + k, i].astype(f32) - centre) * inv_scale * gain_cols[s + k]
                    for k in range(2)
                ]
                ns[0, h, pl.ds(s * channels, 2 * channels), columns(i)] = jnp.concatenate(
                    both, axis=0
                ).astype(bf16)

    def product(h):
        @pl.loop(0, GROUP // 2)
        def _(index):
            pre[half(index)] = jnp.dot(w[0, half(index)], ns[0, h], preferred_element_type=f32)

    def activate(h):
        @pl.loop(0, GROUP * hidden // 32)
        def _(j):
            lines = pl.ds(pl.multiple_of(j * 32, 32), 32)
            value = pre[lines]
            cdf = 0.5 * (1.0 + lax.erf(value * inv_root_two))
            slope = cdf + value * jnp.exp(-0.5 * value * value) * inv_root_two_pi
            ag[1, h, lines] = (value * cdf).astype(bf16)
            ag[0, h, lines] = (gact[h, lines] * slope).astype(bf16)

    def sum_copy(a, h, p, side):
        target = p if side == 0 else jnp.where(p == plane - 1, planes, p)
        return remote(
            red_out.at[a, h, p],
            red_in.at[a, h, target],
            r_send.at[a, h, p],
            r_recv.at[a, h, target],
            {"chan": me + GROUP if side == 0 else me - GROUP},
        )

    def round_out(a, h, p):
        @pl.loop(0, GROUP)
        def _(q):
            for i in range(pc):
                red_out[a, h, p, q, i] = part_sum[a, h, p, q, i].astype(bf16)

    def take(a, h, p, index):
        copy = remote(
            red_out.at[a, h, p],
            red_in.at[a, h, index],
            r_send.at[a, h, p],
            r_recv.at[a, h, index],
            {"chan": lax.rem(me + GROUP, n)},
        )
        copy.wait_recv()

        @pl.loop(0, GROUP)
        def _(q):
            for i in range(pc):
                part_sum[a, h, p, q, i] += red_in[a, h, index, q, i].astype(f32)

    def partial(a, h):
        @pl.loop(0, planes)
        def _(p):
            lines = pl.ds(pl.multiple_of(p * band, band), band)
            result = jnp.dot(wt[a, lines], ag[a, h], preferred_element_type=f32)
            for q in range(GROUP):
                for i in range(pc):
                    part_sum[a, h, p, q, i] = result[
                        q * channels : (q + 1) * channels, i * breadth : (i + 1) * breadth
                    ]

    def emit(a, h):
        @pl.loop(0, planes - 1)
        def _(j):
            @pl.when(plane == 0)
            def _():
                round_out(a, h, planes - 1 - j)
                sum_copy(a, h, planes - 1 - j, 0).start()

            @pl.when(plane == planes - 1)
            def _():
                round_out(a, h, j)
                sum_copy(a, h, j, 1).start()

    def relay(a, h, tau):
        right = planes - 1 - tau + plane

        @pl.when((plane > 0) & (right < planes))
        def _():
            take(a, h, right, right)
            round_out(a, h, right)
            sum_copy(a, h, right, 0).start()

        left = tau - (planes - 1 - plane)

        @pl.when((plane < planes - 1) & (left >= 0))
        def _():
            take(a, h, left, left)
            round_out(a, h, left)
            sum_copy(a, h, left, 1).start()

    def piece_copy(a, h, k):
        return remote(
            red_out.at[a, h, plane, mate(k)],
            piece_in.at[a, pl.ds(lane * part + h * pc, pc)],
            p_send.at[a, h, k],
            p_recv.at[a, h, lane],
            {"chan": plane * GROUP + mate(k)},
        )

    def finals(a, h):
        @pl.when(plane > 0)
        def _():
            take(a, h, plane, plane)

        @pl.when(plane < planes - 1)
        def _():
            take(a, h, plane, planes)

        round_out(a, h, plane)
        for k in range(1, GROUP):
            piece_copy(a, h, k).start()
        for i in range(pc):
            piece_in[a, lane * part + h * pc + i] = red_out[a, h, plane, lane, i]

    def pieces(a, h):
        for k in range(1, GROUP):
            source = mate(k)
            copy = remote(
                red_out.at[a, h, plane, mate(k)],
                piece_in.at[a, pl.ds(source * part + h * pc, pc)],
                p_send.at[a, h, k],
                p_recv.at[a, h, source],
                {"chan": plane * GROUP + mate(k)},
            )
            copy.wait()

    def stats_copy(h, k):
        other = lax.rem(plane + k, planes)
        return remote(
            st_out.at[pl.ds(h * pc, pc)],
            st_in.at[plane, pl.ds(h * pc, pc)],
            s_send.at[h, k],
            s_recv.at[h, plane],
            {"chan": other * GROUP + lane},
        )

    def stats(h):
        @pl.loop(0, pc)
        def _(i):
            centre, inv_scale = st_out[h * pc + i, 2:3], st_out[h * pc + i, 3:4]
            one = jnp.zeros((channels, breadth), f32)
            two = jnp.zeros((channels, breadth), f32)
            for s in range(n):
                gained = part_sum[NORMED, h, s // GROUP, s % GROUP, i] * gain_cols[s]
                one += gained
                two += gained * ((gath[MIXED, h, s, i].astype(f32) - centre) * inv_scale)
            st_out[h * pc + i, 0:1] = jnp.sum(one, axis=0, keepdims=True)
            st_out[h * pc + i, 1:2] = jnp.sum(two, axis=0, keepdims=True)

        for k in range(1, planes):
            stats_copy(h, k).start()

    def stats_total(h):
        for k in range(1, planes):
            source = lax.rem(plane + planes - k, planes)
            copy = remote(
                st_out.at[pl.ds(h * pc, pc)],
                st_in.at[source, pl.ds(h * pc, pc)],
                s_send.at[h, k],
                s_recv.at[h, source],
                {"chan": lax.rem(plane + k, planes) * GROUP + lane},
            )
            copy.wait()
        for i in range(pc):
            here = h * pc + i
            total = st_out[here]
            for k in range(1, planes):
                total += st_in[lax.rem(plane + k, planes), here]
            line = lane * part + here
            st_all[line, 0:2] = total[0:2]
            st_all[line, 2:4] = st_out[here, 2:4]
        for k in range(1, GROUP):
            lines = pl.ds(lane * part + h * pc, pc)
            remote(
                st_all.at[lines],
                st_all.at[lines],
                t_send.at[h, k],
                t_recv.at[h, lane],
                {"chan": plane * GROUP + mate(k)},
            ).start()

    def stats_pieces(h):
        for k in range(1, GROUP):
            source = mate(k)
            copy = remote(
                st_all.at[pl.ds(lane * part + h * pc, pc)],
                st_all.at[pl.ds(source * part + h * pc, pc)],
                t_send.at[h, k],
                t_recv.at[h, source],
                {"chan": plane * GROUP + mate(k)},
            )
            copy.wait()

    contract_tail = (((1,), (1,)), ((), ()))

    def weight_grad(a, index):
        lines = pl.ds(index * hidden, hidden)
        total = lax.dot_general(
            ag[a, 0, lines], ns[a, 0], contract_tail, preferred_element_type=f32
        )
        for h in range(1, CUTS):
            total += lax.dot_general(
                ag[a, h, lines], ns[a, h], contract_tail, preferred_element_type=f32
            )
        return total

    def relays(a, h, start, stop):
        @pl.loop(start, stop)
        def _(tau):
            relay(a, h, tau)

    hops(MIXED, 0, planes - 1)
    normalized(0)
    core_w[0].wait()
    far_w[0].wait()
    turn(0)
    product(0)
    activate(0)
    hops(MIXED, 1, planes - 2)
    hops_between(SCALED, 1, 1, planes - 2)
    partial(NORMED, 0)
    stats(0)
    emit(NORMED, 0)
    partial(BRANCH, 0)
    emit(BRANCH, 0)
    hops(MIXED, 1, planes - 1)
    normalized(1)
    product(1)
    hops(SCALED, 1, planes - 2)
    relay(NORMED, 0, 1)
    hops(SCALED, 1, planes - 1)
    lay_scaled(1)
    back_product(1)
    activate(1)
    partial(NORMED, 1)
    stats(1)
    emit(NORMED, 1)

    def halves(c):
        return c // 2, pl.ds(c % 2 * shorter, shorter)

    def near_grad(c):
        a, lines = halves(c)
        return remote(
            near_out.at[a, lines],
            near_in.at[a, lines],
            pair_send.at[14 + c],
            pair_recv.at[14 + c],
            {"chan": flipped(me, 2)},
        )

    def row_step(c, s):
        a, lines = halves(c)
        index = 18 + 4 * s + c
        return remote(
            row_out.at[s, a, lines],
            row_in.at[s, a, lines],
            pair_send.at[index],
            pair_recv.at[index],
            {"rows": partners[s]},
        )

    def row_begin(c):
        near_grad(c).wait()
        a, first = c // 2, c % 2 * (shorter // 16)

        @pl.loop(first, first + shorter // 16)
        def _(i):
            mine = pl.ds(pl.multiple_of(16 * i, 16), 16)
            row_out[0, a, mine, :] = (
                grads_ref[a][mine, :] + near_in[a, mine, :].astype(f32)
            ).astype(bf16)

        row_step(c, 0).start()

    relays(NORMED, 0, 2, planes - 1)
    core = [None] * 2
    for a in range(2):
        for index in range(2):
            sent[a, pl.ds(index * hidden, hidden)] = weight_grad(a, 2 + index).astype(bf16)
        core[a] = pair(8 + a, sent.at[a], core_in.at[a], {"chan": flipped(me, 1)})
    relay(BRANCH, 0, 1)
    for a in range(2):
        for index in range(2):
            kept[a, pl.ds(index * hidden, hidden)] = weight_grad(a, index)
    finals(NORMED, 0)
    for a in range(2):
        core[a].wait()

        @pl.loop(0, hidden // 16)
        def _(i):
            mine = pl.ds(pl.multiple_of(16 * i, 16), 16)
            other = pl.ds(pl.multiple_of(hidden + 16 * i, 16), 16)
            grads_ref[a][mine, :] = kept[a, mine, :] + core_in[a, mine, :].astype(f32)
            near_out[a, mine, :] = (kept[a, other, :] + core_in[a, other, :].astype(f32)).astype(
                bf16
            )

        if a == 0:
            near_grad(0).start()
            near_grad(1).start()

    relays(BRANCH, 0, 2, planes - 1)
    partial(BRANCH, 1)
    emit(BRANCH, 1)
    relay(NORMED, 1, 1)
    for a in range(2):
        for h in range(CUTS):
            for k in range(1, GROUP):
                spread_copy(a, h, k).wait_send()

            @pl.loop(0, n)
            def _(s):
                home = lax.div(s, GROUP)

                @pl.when(to_right & (home <= plane))
                def _():
                    hop_copy(a, h, s, 0).wait_send()

                @pl.when(to_left & (home >= plane))
                def _():
                    hop_copy(a, h, s, 1).wait_send()

    stats_total(0)
    near_grad(2).start()
    finals(BRANCH, 0)
    relays(NORMED, 1, 2, planes - 1)
    for h in range(1, CUTS):
        stats_total(h)
    row_begin(0)
    finals(NORMED, 1)
    near_grad(3).start()
    row_begin(1)
    for h in range(CUTS):
        stats_pieces(h)
        pieces(NORMED, h)

    sums_one[...] = jnp.zeros_like(sums_one)
    sums_two[...] = jnp.zeros_like(sums_two)

    def normalize(start, stop):
        @pl.loop(start, stop)
        def _(r):
            grad_normed = piece_in[NORMED, r].astype(f32)
            line = st_all[r]
            centre, inv_scale = line[2:3], line[3:4]
            unit = (own[MIXED, r].astype(f32) - centre) * inv_scale
            sums_one[...] += grad_normed * unit
            scaled_grad = grad_normed * gain
            mixed_grad = inv_scale * (
                scaled_grad - line[0:1] * (1.0 / D) - unit * (line[1:2] * (1.0 / D))
            )
            grad_pad[r + 3] = mixed_grad.astype(bf16).astype(f32)

    normalize(0, 3)
    normalize(height - 3, height)
    for i in range(3):
        halo_out[0, i] = grad_pad[3 + i].astype(bf16)
        halo_out[1, i] = grad_pad[height + i].astype(bf16)
    halos = edges(12, halo_out.at[0], halo_out.at[1], halo_in)
    edges_start(*halos)
    normalize(3, height - 3)
    row_begin(2)
    events = planes - 2

    @pl.loop(0, groups)
    def _(g):
        group = pl.ds(pl.multiple_of(8 * g, 8), 8)
        for v in range(KSIZE):
            shifts = [shifted(grad_pad[r + 3, group, :], v - 3) for r in range(height)]
            for u in range(KSIZE):
                both = [shifts[r] * padded[r + u, group, :] for r in range(height)]
                while len(both) > 1:
                    both = [p + q for p, q in zip(both[::2], both[1::2])] + both[
                        len(both) // 2 * 2 :
                    ]
                products[u * KSIZE + v, group, :] = both[0]
        low, high = spaced(g, events, 0)

        @pl.loop(low, high)
        def _(e):
            relay(BRANCH, 1, 1 + e)

        @pl.when(g == groups // 2)
        def _():
            row_begin(3)

    lane_sum = jnp.dot(
        products[...].reshape(KSIZE * KSIZE * channels, breadth),
        jnp.ones((breadth, 128), f32),
        precision=lax.Precision.HIGHEST,
        preferred_element_type=f32,
    ).reshape(KSIZE * KSIZE, channels, 128)
    position = lax.broadcasted_iota(jnp.int32, small_ref.shape, 1)
    taps_grad = jnp.zeros(small_ref.shape, f32)
    for t in range(KSIZE * KSIZE):
        here = t // KSIZE * PITCH + t % KSIZE
        taps_grad = jnp.where(position == here, lane_sum[t], taps_grad)
    small_ref[...] = jnp.where(
        position == TAPS, jnp.sum(sums_one[...], axis=1, keepdims=True), taps_grad
    )

    def exchange(chain, s, value):
        small_out[chain, s] = value
        return pair(
            18 + 4 * steps + chain * steps + s,
            small_out.at[chain, s],
            small_in.at[chain, s],
            {"rows": partners[s]},
        )

    step = exchange(0, 0, small_ref[...])
    finals(BRANCH, 1)
    edges_wait(*halos, halo_in, grad_pad)

    @pl.loop(0, groups)
    def _(g):
        group = pl.ds(pl.multiple_of(8 * g, 8), 8)
        taps = taps_ref[group, :]
        sums = [None] * height
        for v in range(KSIZE):
            shifts = [shifted(grad_pad[r, group, :], v - 3) for r in range(height + 6)]
            for u in range(KSIZE):
                t = u * PITCH + v
                tap = jnp.broadcast_to(taps[:, t : t + 1], taps.shape)
                for r in range(height):
                    term = tap * shifts[r + 6 - u]
                    sums[r] = term if sums[r] is None else sums[r] + term
        total = jnp.stack([sums[r] + cotan[r, group, :] for r in range(height)])
        image_grad_ref[group] = jnp.swapaxes(total, 0, 1).astype(bf16)

    for s in range(steps):
        for c in range(4):
            row_step(c, s).wait()
            final = s == steps - 1
            a, first = c // 2, c % 2 * (shorter // 16)

            @pl.loop(first, first + shorter // 16)
            def _(i):
                mine = pl.ds(pl.multiple_of(16 * i, 16), 16)
                total = row_out[s, a, mine, :].astype(f32) + row_in[s, a, mine, :].astype(f32)
                if final:
                    grads_ref[a][mine, :] = total
                else:
                    row_out[s + 1, a, mine, :] = total.astype(bf16)

            if not final:
                row_step(c, s + 1).start()

    for h in range(CUTS):
        pieces(BRANCH, h)

    @pl.loop(0, height)
    def _(r):
        branch = piece_in[BRANCH, r].astype(f32)
        sums_two[...] += branch * cotan[r]
        running[r] = padded[r + 3] + scale * branch

    @pl.loop(0, groups)
    def _(g):
        group = pl.ds(pl.multiple_of(8 * g, 8), 8)
        block_ref[group] = jnp.swapaxes(running[:, group, :], 0, 1).astype(bf16)

    total = jnp.broadcast_to(jnp.sum(sums_two[...], axis=1, keepdims=True), small_ref.shape)
    last = exchange(1, 0, total)
    small = small_ref[...]
    for s in range(steps):
        step.wait()
        small = small + small_in[0, s]
        if s + 1 < steps:
            step = exchange(0, s + 1, small)
    for s in range(steps):
        last.wait()
        total = total + small_in[1, s]
        if s + 1 < steps:
            last = exchange(1, s + 1, total)
    square[0:channels] = jnp.where(position == TAPS + 1, total, small)
    turned = square[...].T
    for u in range(PITCH):
        packed_ref[u] = turned[u * PITCH : (u + 1) * PITCH, 0:channels]

    for a in range(2):
        for h in range(CUTS):

            @pl.loop(0, planes)
            def _(p):
                @pl.when(p > plane)
                def _():
                    sum_copy(a, h, p, 0).wait_send()

                @pl.when(p < plane)
                def _():
                    sum_copy(a, h, p, 1).wait_send()


def run_block(n, arrays):
    f32, bf16 = jnp.float32, jnp.bfloat16
    channels, height, breadth = arrays[0].shape
    hidden, width = arrays[5].shape
    planes = n // GROUP
    part = height // GROUP
    pc = part // CUTS
    every = GROUP * hidden
    pixels = pc * breadth
    rows = lax.axis_size("rows")
    steps = rows.bit_length() - 1
    pairs = 18 + 6 * steps
    vmem = pl.BlockSpec(memory_space=pltpu.VMEM)
    dma = pltpu.SemaphoreType.DMA
    return pl.pallas_call(
        functools.partial(block_kernel, n, rows),
        out_shape=(
            jax.ShapeDtypeStruct((channels, height, breadth), bf16),
            jax.ShapeDtypeStruct((channels, height, breadth), bf16),
            jax.ShapeDtypeStruct((PITCH, PITCH, channels), f32),
            jax.ShapeDtypeStruct((hidden, width), f32),
            jax.ShapeDtypeStruct((hidden, width), f32),
        ),
        in_specs=[pl.BlockSpec(memory_space=pl.ANY)] * 7,
        out_specs=(vmem,) * 5,
        scratch_shapes=[
            pltpu.VMEM((channels, height, breadth), bf16),
            pltpu.VMEM((channels, height, breadth), bf16),
            pltpu.VMEM((KSIZE, KSIZE, channels), f32),
            pltpu.VMEM((1, channels), f32),
            pltpu.VMEM((1, channels), f32),
            pltpu.VMEM((128, 128), f32),
            pltpu.VMEM((channels, 128), f32),
            pltpu.VMEM((channels, 128), f32),
            pltpu.VMEM((height, channels, breadth), f32),
            pltpu.VMEM((2, 3, channels, breadth), bf16),
            pltpu.VMEM((height + 6, channels, breadth), f32),
            pltpu.VMEM((height, channels, breadth), f32),
            pltpu.VMEM((2, height, channels, breadth), bf16),
            pltpu.VMEM((2, CUTS, n, pc, channels, breadth), bf16),
            pltpu.VMEM((1, 128), f32),
            pltpu.VMEM((n, 1, 128), f32),
            pltpu.VMEM((n, channels, breadth), f32),
            pltpu.VMEM((2, every, width), bf16),
            pltpu.VMEM((2, width, every), bf16),
            pltpu.VMEM((2, CUTS, width, pixels), bf16),
            pltpu.VMEM((CUTS, every, pixels), f32),
            pltpu.VMEM((every, pixels), f32),
            pltpu.VMEM((2, CUTS, every, pixels), bf16),
            pltpu.VMEM((2, CUTS, planes, GROUP, pc, channels, breadth), f32),
            pltpu.VMEM((2, CUTS, planes, GROUP, pc, channels, breadth), bf16),
            pltpu.VMEM((2, CUTS, planes + 1, GROUP, pc, channels, breadth), bf16),
            pltpu.VMEM((2, height, channels, breadth), bf16),
            pltpu.VMEM((part, 4, breadth), f32),
            pltpu.VMEM((planes, part, 4, breadth), f32),
            pltpu.VMEM((height, 4, breadth), f32),
            pltpu.VMEM((2, 2 * hidden, width), f32),
            pltpu.VMEM((2, 2 * hidden, width), bf16),
            pltpu.VMEM((2, 2 * hidden, width), bf16),
            pltpu.VMEM((2, hidden, width), bf16),
            pltpu.VMEM((2, hidden, width), bf16),
            pltpu.VMEM((steps, 2, hidden, width), bf16),
            pltpu.VMEM((steps, 2, hidden, width), bf16),
            pltpu.VMEM((height + 6, channels, breadth), f32),
            pltpu.VMEM((channels, breadth), f32),
            pltpu.VMEM((channels, breadth), f32),
            pltpu.VMEM((KSIZE * KSIZE, channels, breadth), f32),
            pltpu.VMEM((2, 3, channels, breadth), bf16),
            pltpu.VMEM((2, 3, channels, breadth), bf16),
            pltpu.VMEM((2, 3, channels, breadth), bf16),
            pltpu.VMEM((2, steps, channels, 128), f32),
            pltpu.VMEM((2, steps, channels, 128), f32),
            dma((7,)),
            dma((2, CUTS, GROUP)),
            dma((2, CUTS, 2, n)),
            dma((2, CUTS, n)),
            dma((n,)),
            dma((n,)),
            dma((2, CUTS, planes)),
            dma((2, CUTS, planes + 1)),
            dma((2, CUTS, GROUP)),
            dma((2, CUTS, GROUP)),
            dma((CUTS, planes)),
            dma((CUTS, planes)),
            dma((CUTS, GROUP)),
            dma((CUTS, GROUP)),
            dma((pairs,)),
            dma((pairs,)),
        ],
        compiler_params=pltpu.CompilerParams(
            collective_id=0, has_side_effects=True, vmem_limit_bytes=40 * 2**20
        ),
        cost_estimate=pl.CostEstimate(
            flops=4000000000, bytes_accessed=10000000, transcendentals=0
        ),
    )(*arrays)


def body(image, dw_kernel, ln_gain, w_in, w_out, layer_scale, cotangent):
    n = lax.axis_size("chan")
    block_out, image_grad, packed, grad_in, grad_out = run_block(
        n,
        (
            *[
                pltpu.with_memory_space_constraint(value, pltpu.HBM)
                for value in (
                    image[:, 0],
                    cotangent[:, 0],
                    jnp.transpose(dw_kernel, (1, 2, 0)),
                    ln_gain[None, :],
                    layer_scale[None, :],
                    w_in.T,
                    w_out,
                )
            ],
        ),
    )
    return (
        block_out[:, None],
        image_grad[:, None],
        jnp.transpose(packed[:KSIZE, :KSIZE], (2, 0, 1)),
        packed[KSIZE, 0],
        packed[KSIZE, 1],
        grad_in.T,
        grad_out,
    )


def solution(mesh):
    return jax.shard_map(
        body,
        mesh=mesh,
        in_specs=(
            P("chan", None, "rows", None),
            P("chan", None, None),
            P("chan"),
            P(None, "chan"),
            P("chan", None),
            P("chan"),
            P("chan", None, "rows", None),
        ),
        out_specs=(
            P("chan", None, "rows", None),
            P("chan", None, "rows", None),
            P("chan", None, None),
            P("chan"),
            P("chan"),
            P(None, "chan"),
            P("chan", None),
        ),
        check_vma=False,
    )
```

```python
import functools

import jax
import jax.numpy as jnp
from jax import lax
from jax.experimental import pallas as pl
from jax.experimental.pallas import tpu as pltpu
from jax.sharding import PartitionSpec as P

D = 768
KSIZE = 7
PITCH = 8
TAPS = KSIZE * PITCH


epsilon = 1e-06
inv_root_two = 0.7071067811865476
inv_root_two_pi = 0.3989422804014327

GROUP = 4
CUTS = 2
MESH = pl.DeviceIdType.MESH
MIXED, SCALED = 0, 1
NORMED, BRANCH = 0, 1


def shifted(value, shift):
    if shift == 0:
        return value
    breadth = value.shape[1]
    lane = lax.broadcasted_iota(jnp.int32, value.shape, 1)
    rolled = pltpu.roll(value, shift % breadth, 1)
    keep = lane >= shift if shift > 0 else lane < breadth + shift
    return jnp.where(keep, rolled, 0.0)


def flipped(index, bit):
    return index + bit - 2 * bit * lax.rem(lax.div(index, bit), 2)


def block_kernel(
    n,
    rows,
    image_hbm,
    cotan_hbm,
    kernel_hbm,
    gain_hbm,
    scale_hbm,
    w_in_ref,
    w_out_ref,
    block_ref,
    image_grad_ref,
    packed_ref,
    grad_in_ref,
    grad_out_ref,
    image_ref,
    cotan_ref,
    kernel_ref,
    gain_ref,
    scale_ref,
    square,
    taps_ref,
    small_ref,
    cotan,
    image_edge,
    padded,
    running,
    own,
    gath,
    gain_src,
    gain_in,
    gain_cols,
    w,
    wt,
    ns,
    gact,
    pre,
    ag,
    part_sum,
    red_out,
    red_in,
    piece_in,
    st_out,
    st_in,
    st_all,
    kept,
    sent,
    core_in,
    near_out,
    near_in,
    row_out,
    row_in,
    grad_pad,
    sums_one,
    sums_two,
    products,
    image_halo,
    halo_out,
    halo_in,
    small_out,
    small_in,
    in_sem,
    a_send,
    d_send,
    g_send,
    g_recv,
    gain_send,
    gain_recv,
    r_send,
    r_recv,
    p_send,
    p_recv,
    s_send,
    s_recv,
    t_send,
    t_recv,
    pair_send,
    pair_recv,
):
    f32, bf16 = jnp.float32, jnp.bfloat16
    me = lax.axis_index("chan")
    row = lax.axis_index("rows")
    plane, lane = lax.div(me, GROUP), lax.rem(me, GROUP)
    channels, height, breadth = image_ref.shape
    weights, grads_ref = (w_in_ref, w_out_ref), (grad_in_ref, grad_out_ref)
    planes = n // GROUP
    part = height // GROUP
    pc = part // CUTS
    hidden = w_in_ref.shape[0]
    width = w_in_ref.shape[1]
    band = GROUP * channels
    steps = row_out.shape[0]
    groups = channels // 8
    up, down = lax.rem(row + rows - 1, rows), lax.rem(row + 1, rows)
    partners = [flipped(row, 2**s) for s in range(steps)]

    barrier = pltpu.get_barrier_semaphore()
    for k in range(1, n):
        pl.semaphore_signal(
            barrier, inc=1, device_id={"chan": lax.rem(me + k, n)}, device_id_type=MESH
        )
    for other in [up, down] + partners:
        pl.semaphore_signal(barrier, inc=1, device_id={"rows": other}, device_id_type=MESH)

    fetched = [
        (image_hbm, image_ref),
        (cotan_hbm, cotan_ref),
        (kernel_hbm, kernel_ref),
        (gain_hbm, gain_ref),
        (scale_hbm, scale_ref),
        (w_in_ref, w.at[0, pl.ds(0, hidden)]),
        (w_out_ref, w.at[1, pl.ds(0, hidden)]),
    ]
    fetches = [
        pltpu.make_async_copy(source, target, in_sem.at[i])
        for i, (source, target) in enumerate(fetched)
    ]
    for copy in fetches:
        copy.start()

    def remote(source, target, send, recv, device):
        return pltpu.make_async_remote_copy(
            src_ref=source,
            dst_ref=target,
            send_sem=send,
            recv_sem=recv,
            device_id=device,
            device_id_type=MESH,
        )

    def pair(index, source, target, device):
        copy = remote(source, target, pair_send.at[index], pair_recv.at[index], device)
        copy.start()
        return copy

    def mate(k):
        return flipped(flipped(lane, 1), 2) if k == 3 else flipped(lane, k) if k else lane


    def spread_copy(a, h, k):
        lines = pl.ds(mate(k) * part + h * pc, pc)
        return remote(
            own.at[a, lines],
            gath.at[a, h, me],
            a_send.at[a, h, k],
            g_recv.at[a, h, me],
            {"chan": plane * GROUP + mate(k)},
        )

    def hop_copy(a, h, s, side):
        return remote(
            gath.at[a, h, s],
            gath.at[a, h, s],
            g_send.at[a, h, side, s],
            g_recv.at[a, h, s],
            {"chan": me + GROUP if side == 0 else me - GROUP},
        )

    to_right, to_left = plane + 1 < planes, plane >= 1

    def pass_on(a, h, s, side):
        @pl.when(to_right if side == 0 else to_left)
        def _():
            hop_copy(a, h, s, side).start()

    def hop_first(a, h, q):
        s = plane * GROUP + mate(q)
        if not (isinstance(q, int) and q == 0):
            hop_copy(a, h, s, 0).wait_recv()
        pass_on(a, h, s, 0)
        pass_on(a, h, s, 1)

    def hop(a, h, t, q):
        @pl.when(plane >= t)
        def _():
            s = (plane - t) * GROUP + mate(q)
            hop_copy(a, h, s, 0).wait_recv()
            pass_on(a, h, s, 0)

        @pl.when(plane + t < planes)
        def _():
            s = (plane + t) * GROUP + mate(q)
            hop_copy(a, h, s, 1).wait_recv()
            pass_on(a, h, s, 1)

    def diagonal_copy(side, k):
        lines = pl.ds(mate(k) * part, pc)
        target = plane + 1 if side == 0 else plane - 1
        return remote(
            own.at[MIXED, lines],
            gath.at[MIXED, 0, me],
            d_send.at[side, k],
            g_recv.at[MIXED, 0, me],
            {"chan": target * GROUP + mate(k)},
        )

    def diagonals(act):
        for k in range(1, GROUP):

            @pl.when(to_right)
            def _():
                act(diagonal_copy(0, k))

            @pl.when(to_left)
            def _():
                act(diagonal_copy(1, k))

    def hops(a, h, t, which=range(GROUP)):
        for q in which:
            hop(a, h, t, q)

    def hops_between(a, h, start, stop):
        @pl.loop(start, stop)
        def _(t):
            hops(a, h, t)

    def scatter(a, h):
        for k in range(1, GROUP):
            spread_copy(a, h, k).start()

    def firsts(a, h, which=range(GROUP)):
        for q in which:
            hop_first(a, h, q)


    for copy in fetches[2:5]:
        copy.wait()
    square[...] = jnp.zeros_like(square)
    for u in range(KSIZE):
        square[u * PITCH : u * PITCH + KSIZE, 0:channels] = kernel_ref[u]
    square[TAPS : TAPS + 1, 0:channels] = gain_ref[...]
    square[TAPS + 1 : TAPS + 2, 0:channels] = scale_ref[...]
    gain_src[...] = square[TAPS : TAPS + 1]
    taps_ref[...] = square[...].T[:channels]
    scale = jnp.broadcast_to(taps_ref[:, TAPS + 1 : TAPS + 2], (channels, breadth))
    gain = jnp.broadcast_to(taps_ref[:, TAPS : TAPS + 1], (channels, breadth))

    for copy in fetches[:2]:
        copy.wait()

    @pl.loop(0, groups)
    def _(g):
        group = pl.ds(pl.multiple_of(8 * g, 8), 8)
        padded[pl.ds(3, height), group, :] = jnp.swapaxes(image_ref[group].astype(f32), 0, 1)
        cotan[:, group, :] = jnp.swapaxes(cotan_ref[group].astype(f32), 0, 1)

    @pl.loop(0, height)
    def _(r):
        own[SCALED, r] = (scale * cotan[r]).astype(bf16)

    for i in range(3):
        image_edge[0, i] = padded[3 + i].astype(bf16)
        image_edge[1, i] = padded[height + i].astype(bf16)

    def keep_own(a):
        for h in range(CUTS):
            for i in range(pc):
                gath[a, h, me, i] = own[a, lane * part + h * pc + i]

    keep_own(SCALED)
    pl.semaphore_wait(barrier, n + 1 + steps)

    scatter(SCALED, 0)
    firsts(SCALED, 0, [0])

    def edges(index, first, last, arrived):
        return (
            remote(first, arrived.at[1], pair_send.at[index], pair_recv.at[index], {"rows": up}),
            remote(
                last, arrived.at[0], pair_send.at[index + 1], pair_recv.at[index + 1], {"rows": down}
            ),
        )

    def edges_start(upward, downward):
        @pl.when(row > 0)
        def _():
            upward.start()

        @pl.when(row < rows - 1)
        def _():
            downward.start()

    def edges_wait(upward, downward, arrived, target):
        @pl.when(row > 0)
        def _():
            upward.wait_send()
            downward.wait_recv()
            for i in range(3):
                target[i] = arrived[0, i].astype(f32)

        @pl.when(row == 0)
        def _():
            for i in range(3):
                target[i] = jnp.zeros((channels, breadth), f32)

        @pl.when(row < rows - 1)
        def _():
            downward.wait_send()
            upward.wait_recv()
            for i in range(3):
                target[height + 3 + i] = arrived[1, i].astype(f32)

        @pl.when(row == rows - 1)
        def _():
            for i in range(3):
                target[height + 3 + i] = jnp.zeros((channels, breadth), f32)

    image_halos = edges(
        0, image_edge.at[0], image_edge.at[1], image_halo
    )
    edges_start(*image_halos)

    def block(a, index):
        return w.at[a, pl.ds(index * hidden, hidden)]

    core_w, far_w = [None] * 2, [None] * 2
    shorter = hidden // 2
    parity = lax.rem(row, 2)

    def near_rows(a):
        return w.at[a, pl.ds(pl.multiple_of(hidden + parity * shorter, 16), shorter)]

    def near_x(a):
        return remote(
            weights[a].at[pl.ds(pl.multiple_of(parity * shorter, 16), shorter)],
            near_rows(a),
            pair_send.at[2 + a],
            pair_recv.at[2 + a],
            {"chan": flipped(me, 2)},
        )

    def near_y(a):
        return remote(
            near_rows(a),
            near_rows(a),
            pair_send.at[10 + a],
            pair_recv.at[10 + a],
            {"rows": partners[0]},
        )

    def near_on(a):
        near_x(a).wait()
        near_y(a).start()

    near_x(1).start()
    near_x(0).start()
    for a in range(2):
        core_w[a] = pair(4 + a, weights[a], block(a, 2), {"chan": flipped(me, 1)})

    def gain_copy(k):
        return remote(
            gain_src,
            gain_in.at[me],
            gain_send.at[k],
            gain_recv.at[me],
            {"chan": lax.rem(me + k, n)},
        )

    @pl.loop(1, n)
    def _(k):
        gain_copy(k).start()

    gain_in[me] = gain_src[...]
    for copy in fetches[5:]:
        copy.wait()

    firsts(SCALED, 0, [1, 2, 3])
    hops(SCALED, 0, 1, [0, 1])
    edges_wait(*image_halos, image_halo, padded)

    @pl.loop(0, groups)
    def _(g):
        group = pl.ds(pl.multiple_of(8 * g, 8), 8)
        taps = taps_ref[group, :]
        sums = [None] * height
        for v in range(KSIZE):
            shifts = [shifted(padded[r, group, :], 3 - v) for r in range(height + 6)]
            for u in range(KSIZE):
                t = u * PITCH + v
                tap = jnp.broadcast_to(taps[:, t : t + 1], taps.shape)
                for r in range(height):
                    term = tap * shifts[r + u]
                    sums[r] = term if sums[r] is None else sums[r] + term
        for r in range(height):
            running[r, group, :] = sums[r]
    @pl.loop(0, height)
    def _(r):
        own[MIXED, r] = running[r].astype(bf16)

    keep_own(MIXED)
    firsts(MIXED, 0, [0])
    diagonals(lambda copy: copy.start())
    for h in range(CUTS):
        scatter(MIXED, h)
    for h in range(1, CUTS):
        scatter(SCALED, h)
    near_on(1)
    hops(SCALED, 0, 1, [2, 3])
    hops(SCALED, 0, 2, [0, 1])
    hops(SCALED, 0, 2, [2, 3])
    near_on(0)

    @pl.loop(3, planes)
    def _(t):
        hops(SCALED, 0, t)
        hops(MIXED, 0, t - 2)

    firsts(MIXED, 1)
    hops(MIXED, 0, planes - 2)
    firsts(SCALED, 1)
    def far(a):
        near_y(a).wait()
        far_w[a] = pair(6 + a, block(a, 1), block(a, 3), {"chan": flipped(me, 1)})

    far(1)

    def columns(i):
        return pl.ds(pl.multiple_of(i * breadth, breadth), breadth)

    def lay_scaled(h):
        @pl.loop(0, pc)
        def _(i):
            for s in range(0, n, 2):
                both = [gath[SCALED, h, s + k, i].astype(f32) for k in range(2)]
                ns[1, h, pl.ds(s * channels, 2 * channels), columns(i)] = jnp.concatenate(
                    both, axis=0
                ).astype(bf16)

    lay_scaled(0)

    @pl.loop(1, n)
    def _(k):
        copy = remote(
            gain_src,
            gain_in.at[lax.rem(me + n - k, n)],
            gain_send.at[k],
            gain_recv.at[lax.rem(me + n - k, n)],
            {"chan": lax.rem(me + k, n)},
        )
        copy.wait()

    @pl.loop(0, n)
    def _(s):
        square = jnp.broadcast_to(gain_in[s], (breadth, breadth)).T
        gain_cols[s] = square[:channels]

    hops_between(MIXED, 1, 1, planes - 2)
    core_w[1].wait()
    far_w[1].wait()
    double = 2 * hidden

    def half(index):
        return pl.ds(pl.multiple_of(index * double, double), double)

    def back_product(h):
        @pl.loop(0, GROUP // 2)
        def _(index):
            gact[h, half(index)] = jnp.dot(
                w[1, half(index)], ns[1, h], preferred_element_type=f32
            )

    back_product(0)

    def turn(a):
        @pl.loop(0, GROUP * hidden // 128)
        def _(j):
            piece = pl.ds(pl.multiple_of(j * 128, 128), 128)
            wt[a, :, piece] = w[a, piece, :].T

    turn(1)
    far(0)

    def normalized(h):
        @pl.loop(0, pc)
        def _(i):
            total = gath[MIXED, h, 0, i].astype(f32)
            for s in range(1, n):
                total += gath[MIXED, h, s, i].astype(f32)
            centre = jnp.sum(total, axis=0, keepdims=True) * (1.0 / D)
            total = jnp.zeros((channels, breadth), f32)
            for s in range(n):
                total += jnp.square(gath[MIXED, h, s, i].astype(f32) - centre)
            spread = jnp.sum(total, axis=0, keepdims=True) * (1.0 / D)
            inv_scale = lax.rsqrt(spread + epsilon)
            st_out[h * pc + i, 2:3] = centre
            st_out[h * pc + i, 3:4] = inv_scale
            for s in range(0, n, 2):
                both = [
                    (gath[MIXED, h, s + k, i].astype(f32) - centre) * inv_scale * gain_cols[s + k]
                    for k in range(2)
                ]
                ns[0, h, pl.ds(s * channels, 2 * channels), columns(i)] = jnp.concatenate(
                    both, axis=0
                ).astype(bf16)

    def product(h):
        @pl.loop(0, GROUP // 2)
        def _(index):
            pre[half(index)] = jnp.dot(w[0, half(index)], ns[0, h], preferred_element_type=f32)

    def activate(h):
        @pl.loop(0, GROUP * hidden // 32)
        def _(j):
            lines = pl.ds(pl.multiple_of(j * 32, 32), 32)
            value = pre[lines]
            cdf = 0.5 * (1.0 + lax.erf(value * inv_root_two))
            slope = cdf + value * jnp.exp(-0.5 * value * value) * inv_root_two_pi
            ag[1, h, lines] = (value * cdf).astype(bf16)
            ag[0, h, lines] = (gact[h, lines] * slope).astype(bf16)

    def sum_copy(a, h, p, side):
        target = p if side == 0 else jnp.where(p == plane - 1, planes, p)
        return remote(
            red_out.at[a, h, p],
            red_in.at[a, h, target],
            r_send.at[a, h, p],
            r_recv.at[a, h, target],
            {"chan": me + GROUP if side == 0 else me - GROUP},
        )

    def round_out(a, h, p):
        @pl.loop(0, GROUP)
        def _(q):
            for i in range(pc):
                red_out[a, h, p, q, i] = part_sum[a, h, p, q, i].astype(bf16)

    def take(a, h, p, index):
        copy = remote(
            red_out.at[a, h, p],
            red_in.at[a, h, index],
            r_send.at[a, h, p],
            r_recv.at[a, h, index],
            {"chan": lax.rem(me + GROUP, n)},
        )
        copy.wait_recv()

        @pl.loop(0, GROUP)
        def _(q):
            for i in range(pc):
                part_sum[a, h, p, q, i] += red_in[a, h, index, q, i].astype(f32)

    def partial(a, h):
        @pl.loop(0, planes)
        def _(p):
            lines = pl.ds(pl.multiple_of(p * band, band), band)
            result = jnp.dot(wt[a, lines], ag[a, h], preferred_element_type=f32)
            for q in range(GROUP):
                for i in range(pc):
                    part_sum[a, h, p, q, i] = result[
                        q * channels : (q + 1) * channels, i * breadth : (i + 1) * breadth
                    ]

    def emit(a, h):
        @pl.loop(0, planes - 1)
        def _(j):
            @pl.when(plane == 0)
            def _():
                round_out(a, h, planes - 1 - j)
                sum_copy(a, h, planes - 1 - j, 0).start()

            @pl.when(plane == planes - 1)
            def _():
                round_out(a, h, j)
                sum_copy(a, h, j, 1).start()

    def relay(a, h, tau):
        right = planes - 1 - tau + plane

        @pl.when((plane > 0) & (right < planes))
        def _():
            take(a, h, right, right)
            round_out(a, h, right)
            sum_copy(a, h, right, 0).start()

        left = tau - (planes - 1 - plane)

        @pl.when((plane < planes - 1) & (left >= 0))
        def _():
            take(a, h, left, left)
            round_out(a, h, left)
            sum_copy(a, h, left, 1).start()

    def piece_copy(a, h, k):
        return remote(
            red_out.at[a, h, plane, mate(k)],
            piece_in.at[a, pl.ds(lane * part + h * pc, pc)],
            p_send.at[a, h, k],
            p_recv.at[a, h, lane],
            {"chan": plane * GROUP + mate(k)},
        )

    def finals(a, h):
        @pl.when(plane > 0)
        def _():
            take(a, h, plane, plane)

        @pl.when(plane < planes - 1)
        def _():
            take(a, h, plane, planes)

        round_out(a, h, plane)
        for k in range(1, GROUP):
            piece_copy(a, h, k).start()
        for i in range(pc):
            piece_in[a, lane * part + h * pc + i] = red_out[a, h, plane, lane, i]

    def pieces(a, h):
        for k in range(1, GROUP):
            source = mate(k)
            copy = remote(
                red_out.at[a, h, plane, mate(k)],
                piece_in.at[a, pl.ds(source * part + h * pc, pc)],
                p_send.at[a, h, k],
                p_recv.at[a, h, source],
                {"chan": plane * GROUP + mate(k)},
            )
            copy.wait()

    def stats_copy(h, k):
        other = lax.rem(plane + k, planes)
        return remote(
            st_out.at[pl.ds(h * pc, pc)],
            st_in.at[plane, pl.ds(h * pc, pc)],
            s_send.at[h, k],
            s_recv.at[h, plane],
            {"chan": other * GROUP + lane},
        )

    def stats(h):
        @pl.loop(0, pc)
        def _(i):
            centre, inv_scale = st_out[h * pc + i, 2:3], st_out[h * pc + i, 3:4]
            one = jnp.zeros((channels, breadth), f32)
            two = jnp.zeros((channels, breadth), f32)
            for s in range(n):
                gained = part_sum[NORMED, h, s // GROUP, s % GROUP, i] * gain_cols[s]
                one += gained
                two += gained * ((gath[MIXED, h, s, i].astype(f32) - centre) * inv_scale)
            st_out[h * pc + i, 0:1] = jnp.sum(one, axis=0, keepdims=True)
            st_out[h * pc + i, 1:2] = jnp.sum(two, axis=0, keepdims=True)

        for k in range(1, planes):
            stats_copy(h, k).start()

    def stats_total(h):
        for k in range(1, planes):
            source = lax.rem(plane + planes - k, planes)
            copy = remote(
                st_out.at[pl.ds(h * pc, pc)],
                st_in.at[source, pl.ds(h * pc, pc)],
                s_send.at[h, k],
                s_recv.at[h, source],
                {"chan": lax.rem(plane + k, planes) * GROUP + lane},
            )
            copy.wait()
        for i in range(pc):
            here = h * pc + i
            total = st_out[here]
            for k in range(1, planes):
                total += st_in[lax.rem(plane + k, planes), here]
            line = lane * part + here
            st_all[line, 0:2] = total[0:2]
            st_all[line, 2:4] = st_out[here, 2:4]
        for k in range(1, GROUP):
            lines = pl.ds(lane * part + h * pc, pc)
            remote(
                st_all.at[lines],
                st_all.at[lines],
                t_send.at[h, k],
                t_recv.at[h, lane],
                {"chan": plane * GROUP + mate(k)},
            ).start()

    def stats_pieces(h):
        for k in range(1, GROUP):
            source = mate(k)
            copy = remote(
                st_all.at[pl.ds(lane * part + h * pc, pc)],
                st_all.at[pl.ds(source * part + h * pc, pc)],
                t_send.at[h, k],
                t_recv.at[h, source],
                {"chan": plane * GROUP + mate(k)},
            )
            copy.wait()

    contract_tail = (((1,), (1,)), ((), ()))

    def weight_grad(a, index):
        lines = pl.ds(index * hidden, hidden)
        total = lax.dot_general(
            ag[a, 0, lines], ns[a, 0], contract_tail, preferred_element_type=f32
        )
        for h in range(1, CUTS):
            total += lax.dot_general(
                ag[a, h, lines], ns[a, h], contract_tail, preferred_element_type=f32
            )
        return total

    def relays(a, h, start, stop):
        @pl.loop(start, stop)
        def _(tau):
            relay(a, h, tau)

    hops(MIXED, 0, planes - 1)
    for q in range(1, GROUP):
        hop_copy(MIXED, 0, plane * GROUP + mate(q), 0).wait_recv()
    normalized(0)
    core_w[0].wait()
    far_w[0].wait()
    turn(0)
    product(0)
    activate(0)
    hops(MIXED, 1, planes - 2)
    hops_between(SCALED, 1, 1, planes - 2)
    partial(NORMED, 0)
    stats(0)
    emit(NORMED, 0)
    partial(BRANCH, 0)
    emit(BRANCH, 0)
    hops(MIXED, 1, planes - 1)
    normalized(1)
    product(1)
    hops(SCALED, 1, planes - 2)
    relay(NORMED, 0, 1)
    hops(SCALED, 1, planes - 1)
    lay_scaled(1)
    back_product(1)
    activate(1)
    partial(NORMED, 1)
    stats(1)
    emit(NORMED, 1)

    def halves(c):
        return c // 2, pl.ds(c % 2 * shorter, shorter)

    def near_grad(c):
        a, lines = halves(c)
        return remote(
            near_out.at[a, lines],
            near_in.at[a, lines],
            pair_send.at[14 + c],
            pair_recv.at[14 + c],
            {"chan": flipped(me, 2)},
        )

    def row_step(c, s):
        a, lines = halves(c)
        index = 18 + 4 * s + c
        return remote(
            row_out.at[s, a, lines],
            row_in.at[s, a, lines],
            pair_send.at[index],
            pair_recv.at[index],
            {"rows": partners[s]},
        )

    def row_begin(c):
        near_grad(c).wait()
        a, first = c // 2, c % 2 * (shorter // 16)

        @pl.loop(first, first + shorter // 16)
        def _(i):
            mine = pl.ds(pl.multiple_of(16 * i, 16), 16)
            row_out[0, a, mine, :] = (
                grads_ref[a][mine, :] + near_in[a, mine, :].astype(f32)
            ).astype(bf16)

        row_step(c, 0).start()

    relays(NORMED, 0, 2, planes - 1)
    core = [None] * 2
    for a in range(2):
        for index in range(2):
            sent[a, pl.ds(index * hidden, hidden)] = weight_grad(a, 2 + index).astype(bf16)
        core[a] = pair(8 + a, sent.at[a], core_in.at[a], {"chan": flipped(me, 1)})
    relay(BRANCH, 0, 1)
    for a in range(2):
        for index in range(2):
            kept[a, pl.ds(index * hidden, hidden)] = weight_grad(a, index)
    finals(NORMED, 0)
    for a in range(2):
        core[a].wait()

        @pl.loop(0, hidden // 16)
        def _(i):
            mine = pl.ds(pl.multiple_of(16 * i, 16), 16)
            other = pl.ds(pl.multiple_of(hidden + 16 * i, 16), 16)
            grads_ref[a][mine, :] = kept[a, mine, :] + core_in[a, mine, :].astype(f32)
            near_out[a, mine, :] = (kept[a, other, :] + core_in[a, other, :].astype(f32)).astype(
                bf16
            )

        if a == 0:
            near_grad(0).start()
            near_grad(1).start()

    relays(BRANCH, 0, 2, planes - 1)
    partial(BRANCH, 1)
    emit(BRANCH, 1)
    relay(NORMED, 1, 1)
    diagonals(lambda copy: copy.wait_send())
    for a in range(2):
        for h in range(CUTS):
            for k in range(1, GROUP):
                spread_copy(a, h, k).wait_send()

            @pl.loop(0, n)
            def _(s):
                home = lax.div(s, GROUP)
                here = (s == me) if a == MIXED and h == 0 else (home == plane)

                @pl.when(to_right & ((home < plane) | here))
                def _():
                    hop_copy(a, h, s, 0).wait_send()

                @pl.when(to_left & ((home > plane) | here))
                def _():
                    hop_copy(a, h, s, 1).wait_send()

    stats_total(0)
    near_grad(2).start()
    finals(BRANCH, 0)
    near_grad(3).start()
    relays(NORMED, 1, 2, planes - 1)
    for h in range(1, CUTS):
        stats_total(h)
    row_begin(0)
    row_begin(1)
    finals(NORMED, 1)
    relay(BRANCH, 1, 1)
    row_begin(2)
    for h in range(CUTS):
        stats_pieces(h)
        pieces(NORMED, h)

    sums_one[...] = jnp.zeros_like(sums_one)
    sums_two[...] = jnp.zeros_like(sums_two)

    def normalize(start, stop):
        @pl.loop(start, stop)
        def _(r):
            grad_normed = piece_in[NORMED, r].astype(f32)
            line = st_all[r]
            centre, inv_scale = line[2:3], line[3:4]
            unit = (own[MIXED, r].astype(f32) - centre) * inv_scale
            sums_one[...] += grad_normed * unit
            scaled_grad = grad_normed * gain
            mixed_grad = inv_scale * (
                scaled_grad - line[0:1] * (1.0 / D) - unit * (line[1:2] * (1.0 / D))
            )
            grad_pad[r + 3] = mixed_grad.astype(bf16).astype(f32)

    normalize(0, 3)
    normalize(height - 3, height)
    for i in range(3):
        halo_out[0, i] = grad_pad[3 + i].astype(bf16)
        halo_out[1, i] = grad_pad[height + i].astype(bf16)
    halos = edges(12, halo_out.at[0], halo_out.at[1], halo_in)
    edges_start(*halos)
    normalize(3, height - 3)
    row_begin(3)
    @pl.loop(0, groups)
    def _(g):
        group = pl.ds(pl.multiple_of(8 * g, 8), 8)
        for v in range(KSIZE):
            shifts = [shifted(grad_pad[r + 3, group, :], v - 3) for r in range(height)]
            for u in range(KSIZE):
                both = [shifts[r] * padded[r + u, group, :] for r in range(height)]
                while len(both) > 1:
                    both = [p + q for p, q in zip(both[::2], both[1::2])] + both[
                        len(both) // 2 * 2 :
                    ]
                products[u * KSIZE + v, group, :] = both[0]
        @pl.when(g == 1)
        def _():
            relays(BRANCH, 1, 2, planes - 1)


    lane_sum = jnp.dot(
        products[...].reshape(KSIZE * KSIZE * channels, breadth),
        jnp.ones((breadth, 128), f32),
        precision=lax.Precision.HIGHEST,
        preferred_element_type=f32,
    ).reshape(KSIZE * KSIZE, channels, 128)
    position = lax.broadcasted_iota(jnp.int32, small_ref.shape, 1)
    taps_grad = jnp.zeros(small_ref.shape, f32)
    for t in range(KSIZE * KSIZE):
        here = t // KSIZE * PITCH + t % KSIZE
        taps_grad = jnp.where(position == here, lane_sum[t], taps_grad)
    small_ref[...] = jnp.where(
        position == TAPS, jnp.sum(sums_one[...], axis=1, keepdims=True), taps_grad
    )

    def exchange(chain, s, value):
        small_out[chain, s] = value
        return pair(
            18 + 4 * steps + chain * steps + s,
            small_out.at[chain, s],
            small_in.at[chain, s],
            {"rows": partners[s]},
        )

    step = exchange(0, 0, small_ref[...])
    finals(BRANCH, 1)
    edges_wait(*halos, halo_in, grad_pad)

    @pl.loop(0, groups)
    def _(g):
        group = pl.ds(pl.multiple_of(8 * g, 8), 8)
        taps = taps_ref[group, :]
        sums = [None] * height
        for v in range(KSIZE):
            shifts = [shifted(grad_pad[r, group, :], v - 3) for r in range(height + 6)]
            for u in range(KSIZE):
                t = u * PITCH + v
                tap = jnp.broadcast_to(taps[:, t : t + 1], taps.shape)
                for r in range(height):
                    term = tap * shifts[r + 6 - u]
                    sums[r] = term if sums[r] is None else sums[r] + term
        total = jnp.stack([sums[r] + cotan[r, group, :] for r in range(height)])
        image_grad_ref[group] = jnp.swapaxes(total, 0, 1).astype(bf16)

    for h in range(CUTS):
        pieces(BRANCH, h)

    @pl.loop(0, height)
    def _(r):
        branch = piece_in[BRANCH, r].astype(f32)
        sums_two[...] += branch * cotan[r]
        running[r] = padded[r + 3] + scale * branch

    @pl.loop(0, groups)
    def _(g):
        group = pl.ds(pl.multiple_of(8 * g, 8), 8)
        block_ref[group] = jnp.swapaxes(running[:, group, :], 0, 1).astype(bf16)

    total = jnp.broadcast_to(jnp.sum(sums_two[...], axis=1, keepdims=True), small_ref.shape)
    last = exchange(1, 0, total)
    for s in range(steps):
        for c in range(4):
            row_step(c, s).wait()
            final = s == steps - 1
            a, first = c // 2, c % 2 * (shorter // 16)

            @pl.loop(first, first + shorter // 16)
            def _(i):
                mine = pl.ds(pl.multiple_of(16 * i, 16), 16)
                total = row_out[s, a, mine, :].astype(f32) + row_in[s, a, mine, :].astype(f32)
                if final:
                    grads_ref[a][mine, :] = total
                else:
                    row_out[s + 1, a, mine, :] = total.astype(bf16)

            if not final:
                row_step(c, s + 1).start()

    small = small_ref[...]
    for s in range(steps):
        step.wait()
        small = small + small_in[0, s]
        if s + 1 < steps:
            step = exchange(0, s + 1, small)
    for s in range(steps):
        last.wait()
        total = total + small_in[1, s]
        if s + 1 < steps:
            last = exchange(1, s + 1, total)
    square[0:channels] = jnp.where(position == TAPS + 1, total, small)
    turned = square[...].T
    for u in range(PITCH):
        packed_ref[u] = turned[u * PITCH : (u + 1) * PITCH, 0:channels]

    for a in range(2):
        for h in range(CUTS):

            @pl.loop(0, planes)
            def _(p):
                @pl.when(p > plane)
                def _():
                    sum_copy(a, h, p, 0).wait_send()

                @pl.when(p < plane)
                def _():
                    sum_copy(a, h, p, 1).wait_send()


def run_block(n, arrays):
    f32, bf16 = jnp.float32, jnp.bfloat16
    channels, height, breadth = arrays[0].shape
    hidden, width = arrays[5].shape
    planes = n // GROUP
    part = height // GROUP
    pc = part // CUTS
    every = GROUP * hidden
    pixels = pc * breadth
    rows = lax.axis_size("rows")
    steps = rows.bit_length() - 1
    pairs = 18 + 6 * steps
    vmem = pl.BlockSpec(memory_space=pltpu.VMEM)
    dma = pltpu.SemaphoreType.DMA
    return pl.pallas_call(
        functools.partial(block_kernel, n, rows),
        out_shape=(
            jax.ShapeDtypeStruct((channels, height, breadth), bf16),
            jax.ShapeDtypeStruct((channels, height, breadth), bf16),
            jax.ShapeDtypeStruct((PITCH, PITCH, channels), f32),
            jax.ShapeDtypeStruct((hidden, width), f32),
            jax.ShapeDtypeStruct((hidden, width), f32),
        ),
        in_specs=[pl.BlockSpec(memory_space=pl.ANY)] * 7,
        out_specs=(vmem,) * 5,
        scratch_shapes=[
            pltpu.VMEM((channels, height, breadth), bf16),
            pltpu.VMEM((channels, height, breadth), bf16),
            pltpu.VMEM((KSIZE, KSIZE, channels), f32),
            pltpu.VMEM((1, channels), f32),
            pltpu.VMEM((1, channels), f32),
            pltpu.VMEM((128, 128), f32),
            pltpu.VMEM((channels, 128), f32),
            pltpu.VMEM((channels, 128), f32),
            pltpu.VMEM((height, channels, breadth), f32),
            pltpu.VMEM((2, 3, channels, breadth), bf16),
            pltpu.VMEM((height + 6, channels, breadth), f32),
            pltpu.VMEM((height, channels, breadth), f32),
            pltpu.VMEM((2, height, channels, breadth), bf16),
            pltpu.VMEM((2, CUTS, n, pc, channels, breadth), bf16),
            pltpu.VMEM((1, 128), f32),
            pltpu.VMEM((n, 1, 128), f32),
            pltpu.VMEM((n, channels, breadth), f32),
            pltpu.VMEM((2, every, width), bf16),
            pltpu.VMEM((2, width, every), bf16),
            pltpu.VMEM((2, CUTS, width, pixels), bf16),
            pltpu.VMEM((CUTS, every, pixels), f32),
            pltpu.VMEM((every, pixels), f32),
            pltpu.VMEM((2, CUTS, every, pixels), bf16),
            pltpu.VMEM((2, CUTS, planes, GROUP, pc, channels, breadth), f32),
            pltpu.VMEM((2, CUTS, planes, GROUP, pc, channels, breadth), bf16),
            pltpu.VMEM((2, CUTS, planes + 1, GROUP, pc, channels, breadth), bf16),
            pltpu.VMEM((2, height, channels, breadth), bf16),
            pltpu.VMEM((part, 4, breadth), f32),
            pltpu.VMEM((planes, part, 4, breadth), f32),
            pltpu.VMEM((height, 4, breadth), f32),
            pltpu.VMEM((2, 2 * hidden, width), f32),
            pltpu.VMEM((2, 2 * hidden, width), bf16),
            pltpu.VMEM((2, 2 * hidden, width), bf16),
            pltpu.VMEM((2, hidden, width), bf16),
            pltpu.VMEM((2, hidden, width), bf16),
            pltpu.VMEM((steps, 2, hidden, width), bf16),
            pltpu.VMEM((steps, 2, hidden, width), bf16),
            pltpu.VMEM((height + 6, channels, breadth), f32),
            pltpu.VMEM((channels, breadth), f32),
            pltpu.VMEM((channels, breadth), f32),
            pltpu.VMEM((KSIZE * KSIZE, channels, breadth), f32),
            pltpu.VMEM((2, 3, channels, breadth), bf16),
            pltpu.VMEM((2, 3, channels, breadth), bf16),
            pltpu.VMEM((2, 3, channels, breadth), bf16),
            pltpu.VMEM((2, steps, channels, 128), f32),
            pltpu.VMEM((2, steps, channels, 128), f32),
            dma((7,)),
            dma((2, CUTS, GROUP)),
            dma((2, GROUP)),
            dma((2, CUTS, 2, n)),
            dma((2, CUTS, n)),
            dma((n,)),
            dma((n,)),
            dma((2, CUTS, planes)),
            dma((2, CUTS, planes + 1)),
            dma((2, CUTS, GROUP)),
            dma((2, CUTS, GROUP)),
            dma((CUTS, planes)),
            dma((CUTS, planes)),
            dma((CUTS, GROUP)),
            dma((CUTS, GROUP)),
            dma((pairs,)),
            dma((pairs,)),
        ],
        compiler_params=pltpu.CompilerParams(
            collective_id=0, has_side_effects=True, vmem_limit_bytes=40 * 2**20
        ),
        cost_estimate=pl.CostEstimate(
            flops=4000000000, bytes_accessed=10000000, transcendentals=0
        ),
    )(*arrays)


def body(image, dw_kernel, ln_gain, w_in, w_out, layer_scale, cotangent):
    n = lax.axis_size("chan")
    block_out, image_grad, packed, grad_in, grad_out = run_block(
        n,
        (
            *[
                pltpu.with_memory_space_constraint(value, pltpu.HBM)
                for value in (
                    image[:, 0],
                    cotangent[:, 0],
                    jnp.transpose(dw_kernel, (1, 2, 0)),
                    ln_gain[None, :],
                    layer_scale[None, :],
                    w_in.T,
                    w_out,
                )
            ],
        ),
    )
    return (
        block_out[:, None],
        image_grad[:, None],
        jnp.transpose(packed[:KSIZE, :KSIZE], (2, 0, 1)),
        packed[KSIZE, 0],
        packed[KSIZE, 1],
        grad_in.T,
        grad_out,
    )


def solution(mesh):
    return jax.shard_map(
        body,
        mesh=mesh,
        in_specs=(
            P("chan", None, "rows", None),
            P("chan", None, None),
            P("chan"),
            P(None, "chan"),
            P("chan", None),
            P("chan"),
            P("chan", None, "rows", None),
        ),
        out_specs=(
            P("chan", None, "rows", None),
            P("chan", None, "rows", None),
            P("chan", None, None),
            P("chan"),
            P("chan"),
            P(None, "chan"),
            P("chan", None),
        ),
        check_vma=False,
    )
```

```python
import functools

import jax
import jax.numpy as jnp
from jax import lax
from jax.experimental import pallas as pl
from jax.experimental.pallas import tpu as pltpu
from jax.sharding import PartitionSpec as P

D = 768
KSIZE = 7
PITCH = 8
TAPS = KSIZE * PITCH


epsilon = 1e-06
inv_root_two = 0.7071067811865476
inv_root_two_pi = 0.3989422804014327

GROUP = 4
CUTS = 2
MESH = pl.DeviceIdType.MESH
MIXED, SCALED = 0, 1
NORMED, BRANCH = 0, 1


def shifted(value, shift):
    if shift == 0:
        return value
    breadth = value.shape[1]
    lane = lax.broadcasted_iota(jnp.int32, value.shape, 1)
    rolled = pltpu.roll(value, shift % breadth, 1)
    keep = lane >= shift if shift > 0 else lane < breadth + shift
    return jnp.where(keep, rolled, 0.0)


def flipped(index, bit):
    return index + bit - 2 * bit * lax.rem(lax.div(index, bit), 2)


def block_kernel(
    n,
    rows,
    image_hbm,
    cotan_hbm,
    kernel_hbm,
    gain_hbm,
    scale_hbm,
    w_in_ref,
    w_out_ref,
    block_ref,
    image_grad_ref,
    packed_ref,
    grad_in_ref,
    grad_out_ref,
    image_ref,
    cotan_ref,
    kernel_ref,
    gain_ref,
    scale_ref,
    square,
    taps_ref,
    small_ref,
    cotan,
    image_edge,
    padded,
    running,
    own,
    gath,
    gain_src,
    gain_in,
    gain_cols,
    w,
    wt,
    ns,
    gact,
    pre,
    ag,
    part_sum,
    red_out,
    red_in,
    piece_in,
    st_out,
    st_in,
    st_all,
    kept,
    sent,
    core_in,
    near_out,
    near_in,
    row_out,
    row_in,
    grad_pad,
    sums_one,
    sums_two,
    products,
    image_halo,
    halo_out,
    halo_in,
    small_out,
    small_in,
    in_sem,
    a_send,
    d_send,
    g_send,
    g_recv,
    gain_send,
    gain_recv,
    r_send,
    r_recv,
    p_send,
    p_recv,
    s_send,
    s_recv,
    t_send,
    t_recv,
    pair_send,
    pair_recv,
):
    f32, bf16 = jnp.float32, jnp.bfloat16
    me = lax.axis_index("chan")
    row = lax.axis_index("rows")
    plane, lane = lax.div(me, GROUP), lax.rem(me, GROUP)
    channels, height, breadth = image_ref.shape
    weights, grads_ref = (w_in_ref, w_out_ref), (grad_in_ref, grad_out_ref)
    planes = n // GROUP
    part = height // GROUP
    pc = part // CUTS
    hidden = w_in_ref.shape[0]
    width = w_in_ref.shape[1]
    band = GROUP * channels
    steps = row_out.shape[0]
    groups = channels // 8
    up, down = lax.rem(row + rows - 1, rows), lax.rem(row + 1, rows)
    partners = [flipped(row, 2**s) for s in range(steps)]

    barrier = pltpu.get_barrier_semaphore()
    for k in range(1, n):
        pl.semaphore_signal(
            barrier, inc=1, device_id={"chan": lax.rem(me + k, n)}, device_id_type=MESH
        )
    for other in [up, down] + partners:
        pl.semaphore_signal(barrier, inc=1, device_id={"rows": other}, device_id_type=MESH)

    fetched = [
        (image_hbm, image_ref),
        (cotan_hbm, cotan_ref),
        (kernel_hbm, kernel_ref),
        (gain_hbm, gain_ref),
        (scale_hbm, scale_ref),
        (w_in_ref, w.at[0, pl.ds(0, hidden)]),
        (w_out_ref, w.at[1, pl.ds(0, hidden)]),
    ]
    fetches = [
        pltpu.make_async_copy(source, target, in_sem.at[i])
        for i, (source, target) in enumerate(fetched)
    ]
    for copy in fetches:
        copy.start()

    def remote(source, target, send, recv, device):
        return pltpu.make_async_remote_copy(
            src_ref=source,
            dst_ref=target,
            send_sem=send,
            recv_sem=recv,
            device_id=device,
            device_id_type=MESH,
        )

    def pair(index, source, target, device):
        copy = remote(source, target, pair_send.at[index], pair_recv.at[index], device)
        copy.start()
        return copy

    def mate(k):
        return flipped(flipped(lane, 1), 2) if k == 3 else flipped(lane, k) if k else lane


    def spread_copy(a, h, k):
        lines = pl.ds(mate(k) * part + h * pc, pc)
        return remote(
            own.at[a, lines],
            gath.at[a, h, me],
            a_send.at[a, h, k],
            g_recv.at[a, h, me],
            {"chan": plane * GROUP + mate(k)},
        )

    def hop_copy(a, h, s, side):
        return remote(
            gath.at[a, h, s],
            gath.at[a, h, s],
            g_send.at[a, h, side, s],
            g_recv.at[a, h, s],
            {"chan": me + GROUP if side == 0 else me - GROUP},
        )

    to_right, to_left = plane + 1 < planes, plane >= 1

    def pass_on(a, h, s, side):
        @pl.when(to_right if side == 0 else to_left)
        def _():
            hop_copy(a, h, s, side).start()

    def hop_first(a, h, q):
        s = plane * GROUP + mate(q)
        if not (isinstance(q, int) and q == 0):
            hop_copy(a, h, s, 0).wait_recv()
        pass_on(a, h, s, 0)
        pass_on(a, h, s, 1)

    def hop(a, h, t, q):
        @pl.when(plane >= t)
        def _():
            s = (plane - t) * GROUP + mate(q)
            hop_copy(a, h, s, 0).wait_recv()
            pass_on(a, h, s, 0)

        @pl.when(plane + t < planes)
        def _():
            s = (plane + t) * GROUP + mate(q)
            hop_copy(a, h, s, 1).wait_recv()
            pass_on(a, h, s, 1)

    def diagonal_copy(side, k):
        lines = pl.ds(mate(k) * part, pc)
        target = plane + 1 if side == 0 else plane - 1
        return remote(
            own.at[MIXED, lines],
            gath.at[MIXED, 0, me],
            d_send.at[side, k],
            g_recv.at[MIXED, 0, me],
            {"chan": target * GROUP + mate(k)},
        )

    def diagonals(act):
        for k in range(1, GROUP):

            @pl.when(to_right)
            def _():
                act(diagonal_copy(0, k))

            @pl.when(to_left)
            def _():
                act(diagonal_copy(1, k))

    def hops(a, h, t, which=range(GROUP)):
        for q in which:
            hop(a, h, t, q)

    def hops_between(a, h, start, stop):
        @pl.loop(start, stop)
        def _(t):
            hops(a, h, t)

    def scatter(a, h):
        for k in range(1, GROUP):
            spread_copy(a, h, k).start()

    def firsts(a, h, which=range(GROUP)):
        for q in which:
            hop_first(a, h, q)


    for copy in fetches[2:5]:
        copy.wait()
    square[...] = jnp.zeros_like(square)
    for u in range(KSIZE):
        square[u * PITCH : u * PITCH + KSIZE, 0:channels] = kernel_ref[u]
    square[TAPS : TAPS + 1, 0:channels] = gain_ref[...]
    square[TAPS + 1 : TAPS + 2, 0:channels] = scale_ref[...]
    gain_src[...] = square[TAPS : TAPS + 1]
    taps_ref[...] = square[...].T[:channels]
    scale = jnp.broadcast_to(taps_ref[:, TAPS + 1 : TAPS + 2], (channels, breadth))
    gain = jnp.broadcast_to(taps_ref[:, TAPS : TAPS + 1], (channels, breadth))

    for copy in fetches[:2]:
        copy.wait()

    @pl.loop(0, groups)
    def _(g):
        group = pl.ds(pl.multiple_of(8 * g, 8), 8)
        padded[pl.ds(3, height), group, :] = jnp.swapaxes(image_ref[group].astype(f32), 0, 1)
        cotan[:, group, :] = jnp.swapaxes(cotan_ref[group].astype(f32), 0, 1)

    @pl.loop(0, height)
    def _(r):
        own[SCALED, r] = (scale * cotan[r]).astype(bf16)

    for i in range(3):
        image_edge[0, i] = padded[3 + i].astype(bf16)
        image_edge[1, i] = padded[height + i].astype(bf16)

    def keep_own(a):
        for h in range(CUTS):
            for i in range(pc):
                gath[a, h, me, i] = own[a, lane * part + h * pc + i]

    keep_own(SCALED)
    pl.semaphore_wait(barrier, n + 1 + steps)

    scatter(SCALED, 0)
    firsts(SCALED, 0, [0])

    def edges(index, first, last, arrived):
        return (
            remote(first, arrived.at[1], pair_send.at[index], pair_recv.at[index], {"rows": up}),
            remote(
                last, arrived.at[0], pair_send.at[index + 1], pair_recv.at[index + 1], {"rows": down}
            ),
        )

    def edges_start(upward, downward):
        @pl.when(row > 0)
        def _():
            upward.start()

        @pl.when(row < rows - 1)
        def _():
            downward.start()

    def edges_wait(upward, downward, arrived, target):
        @pl.when(row > 0)
        def _():
            upward.wait_send()
            downward.wait_recv()
            for i in range(3):
                target[i] = arrived[0, i].astype(f32)

        @pl.when(row == 0)
        def _():
            for i in range(3):
                target[i] = jnp.zeros((channels, breadth), f32)

        @pl.when(row < rows - 1)
        def _():
            downward.wait_send()
            upward.wait_recv()
            for i in range(3):
                target[height + 3 + i] = arrived[1, i].astype(f32)

        @pl.when(row == rows - 1)
        def _():
            for i in range(3):
                target[height + 3 + i] = jnp.zeros((channels, breadth), f32)

    image_halos = edges(
        0, image_edge.at[0], image_edge.at[1], image_halo
    )
    edges_start(*image_halos)

    def block(a, index):
        return w.at[a, pl.ds(index * hidden, hidden)]

    core_w, far_w = [None] * 2, [None] * 2
    shorter = hidden // 2
    parity = lax.rem(row, 2)

    def near_rows(a):
        return w.at[a, pl.ds(pl.multiple_of(hidden + parity * shorter, 16), shorter)]

    def near_x(a):
        return remote(
            weights[a].at[pl.ds(pl.multiple_of(parity * shorter, 16), shorter)],
            near_rows(a),
            pair_send.at[2 + a],
            pair_recv.at[2 + a],
            {"chan": flipped(me, 2)},
        )

    def near_y(a):
        return remote(
            near_rows(a),
            near_rows(a),
            pair_send.at[10 + a],
            pair_recv.at[10 + a],
            {"rows": partners[0]},
        )

    def near_on(a):
        near_x(a).wait()
        near_y(a).start()

    near_x(1).start()
    near_x(0).start()
    for a in range(2):
        core_w[a] = pair(4 + a, weights[a], block(a, 2), {"chan": flipped(me, 1)})

    def gain_copy(k):
        return remote(
            gain_src,
            gain_in.at[me],
            gain_send.at[k],
            gain_recv.at[me],
            {"chan": lax.rem(me + k, n)},
        )

    @pl.loop(1, n)
    def _(k):
        gain_copy(k).start()

    gain_in[me] = gain_src[...]
    for copy in fetches[5:]:
        copy.wait()

    firsts(SCALED, 0, [1, 2, 3])
    hops(SCALED, 0, 1, [0, 1])
    edges_wait(*image_halos, image_halo, padded)

    @pl.loop(0, groups)
    def _(g):
        group = pl.ds(pl.multiple_of(8 * g, 8), 8)
        taps = taps_ref[group, :]
        sums = [None] * height
        for v in range(KSIZE):
            shifts = [shifted(padded[r, group, :], 3 - v) for r in range(height + 6)]
            for u in range(KSIZE):
                t = u * PITCH + v
                tap = jnp.broadcast_to(taps[:, t : t + 1], taps.shape)
                for r in range(height):
                    term = tap * shifts[r + u]
                    sums[r] = term if sums[r] is None else sums[r] + term
        for r in range(height):
            running[r, group, :] = sums[r]
    @pl.loop(0, height)
    def _(r):
        own[MIXED, r] = running[r].astype(bf16)

    keep_own(MIXED)
    firsts(MIXED, 0, [0])
    diagonals(lambda copy: copy.start())
    for h in range(CUTS):
        scatter(MIXED, h)
    for h in range(1, CUTS):
        scatter(SCALED, h)
    near_on(1)
    hops(SCALED, 0, 1, [2, 3])
    hops(SCALED, 0, 2, [0, 1])
    hops(SCALED, 0, 2, [2, 3])
    near_on(0)

    @pl.loop(3, planes)
    def _(t):
        hops(SCALED, 0, t)
        hops(MIXED, 0, t - 2)

    firsts(MIXED, 1)
    hops(MIXED, 0, planes - 2)
    firsts(SCALED, 1)
    def far(a):
        near_y(a).wait()
        far_w[a] = pair(6 + a, block(a, 1), block(a, 3), {"chan": flipped(me, 1)})

    far(1)

    def columns(i):
        return pl.ds(pl.multiple_of(i * breadth, breadth), breadth)

    def lay_scaled(h):
        @pl.loop(0, pc)
        def _(i):
            for s in range(0, n, 2):
                both = [gath[SCALED, h, s + k, i].astype(f32) for k in range(2)]
                ns[1, h, pl.ds(s * channels, 2 * channels), columns(i)] = jnp.concatenate(
                    both, axis=0
                ).astype(bf16)

    lay_scaled(0)

    @pl.loop(1, n)
    def _(k):
        copy = remote(
            gain_src,
            gain_in.at[lax.rem(me + n - k, n)],
            gain_send.at[k],
            gain_recv.at[lax.rem(me + n - k, n)],
            {"chan": lax.rem(me + k, n)},
        )
        copy.wait()

    @pl.loop(0, n)
    def _(s):
        square = jnp.broadcast_to(gain_in[s], (breadth, breadth)).T
        gain_cols[s] = square[:channels]

    hops_between(MIXED, 1, 1, planes - 2)
    core_w[1].wait()
    far_w[1].wait()
    double = 2 * hidden

    def half(index):
        return pl.ds(pl.multiple_of(index * double, double), double)

    def back_product(h):
        @pl.loop(0, GROUP // 2)
        def _(index):
            gact[h, half(index)] = jnp.dot(
                w[1, half(index)], ns[1, h], preferred_element_type=f32
            )

    back_product(0)

    def turn(a):
        @pl.loop(0, GROUP * hidden // 128)
        def _(j):
            piece = pl.ds(pl.multiple_of(j * 128, 128), 128)
            wt[a, :, piece] = w[a, piece, :].T

    turn(1)
    far(0)

    def normalized(h):
        @pl.loop(0, pc)
        def _(i):
            total = gath[MIXED, h, 0, i].astype(f32)
            for s in range(1, n):
                total += gath[MIXED, h, s, i].astype(f32)
            centre = jnp.sum(total, axis=0, keepdims=True) * (1.0 / D)
            total = jnp.zeros((channels, breadth), f32)
            for s in range(n):
                total += jnp.square(gath[MIXED, h, s, i].astype(f32) - centre)
            spread = jnp.sum(total, axis=0, keepdims=True) * (1.0 / D)
            inv_scale = lax.rsqrt(spread + epsilon)
            st_out[h * pc + i, 2:3] = centre
            st_out[h * pc + i, 3:4] = inv_scale
            for s in range(0, n, 2):
                both = [
                    (gath[MIXED, h, s + k, i].astype(f32) - centre) * inv_scale * gain_cols[s + k]
                    for k in range(2)
                ]
                ns[0, h, pl.ds(s * channels, 2 * channels), columns(i)] = jnp.concatenate(
                    both, axis=0
                ).astype(bf16)

    def product(h):
        @pl.loop(0, GROUP // 2)
        def _(index):
            pre[half(index)] = jnp.dot(w[0, half(index)], ns[0, h], preferred_element_type=f32)

    def activate(h):
        @pl.loop(0, GROUP * hidden // 32)
        def _(j):
            lines = pl.ds(pl.multiple_of(j * 32, 32), 32)
            value = pre[lines]
            cdf = 0.5 * (1.0 + lax.erf(value * inv_root_two))
            slope = cdf + value * jnp.exp(-0.5 * value * value) * inv_root_two_pi
            ag[1, h, lines] = (value * cdf).astype(bf16)
            ag[0, h, lines] = (gact[h, lines] * slope).astype(bf16)

    def sum_copy(a, h, p, side):
        target = p if side == 0 else jnp.where(p == plane - 1, planes, p)
        return remote(
            red_out.at[a, h, p],
            red_in.at[a, h, target],
            r_send.at[a, h, p],
            r_recv.at[a, h, target],
            {"chan": me + GROUP if side == 0 else me - GROUP},
        )

    def round_out(a, h, p):
        @pl.loop(0, GROUP)
        def _(q):
            for i in range(pc):
                red_out[a, h, p, q, i] = part_sum[a, h, p, q, i].astype(bf16)

    def take(a, h, p, index):
        copy = remote(
            red_out.at[a, h, p],
            red_in.at[a, h, index],
            r_send.at[a, h, p],
            r_recv.at[a, h, index],
            {"chan": lax.rem(me + GROUP, n)},
        )
        copy.wait_recv()

        @pl.loop(0, GROUP)
        def _(q):
            for i in range(pc):
                part_sum[a, h, p, q, i] += red_in[a, h, index, q, i].astype(f32)

    def partial(a, h):
        @pl.loop(0, planes)
        def _(p):
            lines = pl.ds(pl.multiple_of(p * band, band), band)
            result = jnp.dot(wt[a, lines], ag[a, h], preferred_element_type=f32)
            for q in range(GROUP):
                for i in range(pc):
                    part_sum[a, h, p, q, i] = result[
                        q * channels : (q + 1) * channels, i * breadth : (i + 1) * breadth
                    ]

    def emit(a, h):
        @pl.loop(0, planes - 1)
        def _(j):
            @pl.when(plane == 0)
            def _():
                round_out(a, h, planes - 1 - j)
                sum_copy(a, h, planes - 1 - j, 0).start()

            @pl.when(plane == planes - 1)
            def _():
                round_out(a, h, j)
                sum_copy(a, h, j, 1).start()

    def relay(a, h, tau):
        right = planes - 1 - tau + plane

        @pl.when((plane > 0) & (right < planes))
        def _():
            take(a, h, right, right)
            round_out(a, h, right)
            sum_copy(a, h, right, 0).start()

        left = tau - (planes - 1 - plane)

        @pl.when((plane < planes - 1) & (left >= 0))
        def _():
            take(a, h, left, left)
            round_out(a, h, left)
            sum_copy(a, h, left, 1).start()

    def piece_copy(a, h, k):
        return remote(
            red_out.at[a, h, plane, mate(k)],
            piece_in.at[a, pl.ds(lane * part + h * pc, pc)],
            p_send.at[a, h, k],
            p_recv.at[a, h, lane],
            {"chan": plane * GROUP + mate(k)},
        )

    def finals(a, h):
        @pl.when(plane > 0)
        def _():
            take(a, h, plane, plane)

        @pl.when(plane < planes - 1)
        def _():
            take(a, h, plane, planes)

        round_out(a, h, plane)
        for k in range(1, GROUP):
            piece_copy(a, h, k).start()
        for i in range(pc):
            piece_in[a, lane * part + h * pc + i] = red_out[a, h, plane, lane, i]

    def pieces(a, h):
        for k in range(1, GROUP):
            source = mate(k)
            copy = remote(
                red_out.at[a, h, plane, mate(k)],
                piece_in.at[a, pl.ds(source * part + h * pc, pc)],
                p_send.at[a, h, k],
                p_recv.at[a, h, source],
                {"chan": plane * GROUP + mate(k)},
            )
            copy.wait()

    def stats_copy(h, k):
        other = lax.rem(plane + k, planes)
        return remote(
            st_out.at[pl.ds(h * pc, pc)],
            st_in.at[plane, pl.ds(h * pc, pc)],
            s_send.at[h, k],
            s_recv.at[h, plane],
            {"chan": other * GROUP + lane},
        )

    def stats(h):
        @pl.loop(0, pc)
        def _(i):
            centre, inv_scale = st_out[h * pc + i, 2:3], st_out[h * pc + i, 3:4]
            one = jnp.zeros((channels, breadth), f32)
            two = jnp.zeros((channels, breadth), f32)
            for s in range(n):
                gained = part_sum[NORMED, h, s // GROUP, s % GROUP, i] * gain_cols[s]
                one += gained
                two += gained * ((gath[MIXED, h, s, i].astype(f32) - centre) * inv_scale)
            st_out[h * pc + i, 0:1] = jnp.sum(one, axis=0, keepdims=True)
            st_out[h * pc + i, 1:2] = jnp.sum(two, axis=0, keepdims=True)

        for k in range(1, planes):
            stats_copy(h, k).start()

    def stats_total(h):
        for k in range(1, planes):
            source = lax.rem(plane + planes - k, planes)
            copy = remote(
                st_out.at[pl.ds(h * pc, pc)],
                st_in.at[source, pl.ds(h * pc, pc)],
                s_send.at[h, k],
                s_recv.at[h, source],
                {"chan": lax.rem(plane + k, planes) * GROUP + lane},
            )
            copy.wait()
        for i in range(pc):
            here = h * pc + i
            total = st_out[here]
            for k in range(1, planes):
                total += st_in[lax.rem(plane + k, planes), here]
            line = lane * part + here
            st_all[line, 0:2] = total[0:2]
            st_all[line, 2:4] = st_out[here, 2:4]
        for k in range(1, GROUP):
            lines = pl.ds(lane * part + h * pc, pc)
            remote(
                st_all.at[lines],
                st_all.at[lines],
                t_send.at[h, k],
                t_recv.at[h, lane],
                {"chan": plane * GROUP + mate(k)},
            ).start()

    def stats_pieces(h):
        for k in range(1, GROUP):
            source = mate(k)
            copy = remote(
                st_all.at[pl.ds(lane * part + h * pc, pc)],
                st_all.at[pl.ds(source * part + h * pc, pc)],
                t_send.at[h, k],
                t_recv.at[h, source],
                {"chan": plane * GROUP + mate(k)},
            )
            copy.wait()

    contract_tail = (((1,), (1,)), ((), ()))

    def weight_grad(a, index):
        lines = pl.ds(index * hidden, hidden)
        total = lax.dot_general(
            ag[a, 0, lines], ns[a, 0], contract_tail, preferred_element_type=f32
        )
        for h in range(1, CUTS):
            total += lax.dot_general(
                ag[a, h, lines], ns[a, h], contract_tail, preferred_element_type=f32
            )
        return total

    def relays(a, h, start, stop):
        @pl.loop(start, stop)
        def _(tau):
            relay(a, h, tau)

    hops(MIXED, 0, planes - 1)
    for q in range(1, GROUP):
        hop_copy(MIXED, 0, plane * GROUP + mate(q), 0).wait_recv()
    normalized(0)
    core_w[0].wait()
    far_w[0].wait()
    turn(0)
    product(0)
    activate(0)
    hops(MIXED, 1, planes - 2)
    hops_between(SCALED, 1, 1, planes - 2)
    partial(NORMED, 0)
    stats(0)
    emit(NORMED, 0)
    partial(BRANCH, 0)
    emit(BRANCH, 0)
    hops(MIXED, 1, planes - 1)
    normalized(1)
    product(1)
    hops(SCALED, 1, planes - 2)
    relay(NORMED, 0, 1)
    hops(SCALED, 1, planes - 1)
    lay_scaled(1)
    back_product(1)
    activate(1)
    partial(NORMED, 1)
    stats(1)
    emit(NORMED, 1)

    def halves(c):
        return c // 2, pl.ds(c % 2 * shorter, shorter)

    def near_grad(c):
        a, lines = halves(c)
        return remote(
            near_out.at[a, lines],
            near_in.at[a, lines],
            pair_send.at[14 + c],
            pair_recv.at[14 + c],
            {"chan": flipped(me, 2)},
        )

    def row_step(c, s):
        a, lines = halves(c)
        index = 18 + 4 * s + c
        return remote(
            row_out.at[s, a, lines],
            row_in.at[s, a, lines],
            pair_send.at[index],
            pair_recv.at[index],
            {"rows": partners[s]},
        )

    def row_begin(c):
        near_grad(c).wait()
        a, first = c // 2, c % 2 * (shorter // 16)

        @pl.loop(first, first + shorter // 16)
        def _(i):
            mine = pl.ds(pl.multiple_of(16 * i, 16), 16)
            row_out[0, a, mine, :] = (
                grads_ref[a][mine, :] + near_in[a, mine, :].astype(f32)
            ).astype(bf16)

        row_step(c, 0).start()

    relays(NORMED, 0, 2, planes - 1)
    core = [None] * 2
    for a in range(2):
        for index in range(2):
            sent[a, pl.ds(index * hidden, hidden)] = weight_grad(a, 2 + index).astype(bf16)
        core[a] = pair(8 + a, sent.at[a], core_in.at[a], {"chan": flipped(me, 1)})
    relay(BRANCH, 0, 1)
    for a in range(2):
        for index in range(2):
            kept[a, pl.ds(index * hidden, hidden)] = weight_grad(a, index)
    finals(NORMED, 0)
    for a in range(2):
        core[a].wait()

        @pl.loop(0, hidden // 16)
        def _(i):
            mine = pl.ds(pl.multiple_of(16 * i, 16), 16)
            other = pl.ds(pl.multiple_of(hidden + 16 * i, 16), 16)
            grads_ref[a][mine, :] = kept[a, mine, :] + core_in[a, mine, :].astype(f32)
            near_out[a, mine, :] = (kept[a, other, :] + core_in[a, other, :].astype(f32)).astype(
                bf16
            )

        if a == 0:
            near_grad(0).start()
            near_grad(1).start()

    relays(BRANCH, 0, 2, planes - 1)
    partial(BRANCH, 1)
    emit(BRANCH, 1)
    relay(NORMED, 1, 1)
    diagonals(lambda copy: copy.wait_send())
    for a in range(2):
        for h in range(CUTS):
            for k in range(1, GROUP):
                spread_copy(a, h, k).wait_send()

            @pl.loop(0, n)
            def _(s):
                home = lax.div(s, GROUP)
                here = (s == me) if a == MIXED and h == 0 else (home == plane)

                @pl.when(to_right & ((home < plane) | here))
                def _():
                    hop_copy(a, h, s, 0).wait_send()

                @pl.when(to_left & ((home > plane) | here))
                def _():
                    hop_copy(a, h, s, 1).wait_send()

    stats_total(0)
    near_grad(2).start()
    finals(BRANCH, 0)
    near_grad(3).start()
    relays(NORMED, 1, 2, planes - 1)
    for h in range(1, CUTS):
        stats_total(h)
    row_begin(0)
    row_begin(1)
    relay(BRANCH, 1, 1)
    finals(NORMED, 1)
    row_begin(2)
    for h in range(CUTS):
        stats_pieces(h)
        pieces(NORMED, h)

    sums_one[...] = jnp.zeros_like(sums_one)
    sums_two[...] = jnp.zeros_like(sums_two)

    def normalize(start, stop):
        @pl.loop(start, stop)
        def _(r):
            grad_normed = piece_in[NORMED, r].astype(f32)
            line = st_all[r]
            centre, inv_scale = line[2:3], line[3:4]
            unit = (own[MIXED, r].astype(f32) - centre) * inv_scale
            sums_one[...] += grad_normed * unit
            scaled_grad = grad_normed * gain
            mixed_grad = inv_scale * (
                scaled_grad - line[0:1] * (1.0 / D) - unit * (line[1:2] * (1.0 / D))
            )
            grad_pad[r + 3] = mixed_grad.astype(bf16).astype(f32)

    normalize(0, 3)
    normalize(height - 3, height)
    for i in range(3):
        halo_out[0, i] = grad_pad[3 + i].astype(bf16)
        halo_out[1, i] = grad_pad[height + i].astype(bf16)
    halos = edges(12, halo_out.at[0], halo_out.at[1], halo_in)
    edges_start(*halos)
    normalize(3, height - 3)
    row_begin(3)
    relays(BRANCH, 1, 2, planes - 1)
    @pl.loop(0, groups)
    def _(g):
        group = pl.ds(pl.multiple_of(8 * g, 8), 8)
        for v in range(KSIZE):
            shifts = [shifted(grad_pad[r + 3, group, :], v - 3) for r in range(height)]
            for u in range(KSIZE):
                both = [shifts[r] * padded[r + u, group, :] for r in range(height)]
                while len(both) > 1:
                    both = [p + q for p, q in zip(both[::2], both[1::2])] + both[
                        len(both) // 2 * 2 :
                    ]
                products[u * KSIZE + v, group, :] = both[0]

    lane_sum = jnp.dot(
        products[...].reshape(KSIZE * KSIZE * channels, breadth),
        jnp.ones((breadth, 128), f32),
        precision=lax.Precision.HIGHEST,
        preferred_element_type=f32,
    ).reshape(KSIZE * KSIZE, channels, 128)
    position = lax.broadcasted_iota(jnp.int32, small_ref.shape, 1)
    taps_grad = jnp.zeros(small_ref.shape, f32)
    for t in range(KSIZE * KSIZE):
        here = t // KSIZE * PITCH + t % KSIZE
        taps_grad = jnp.where(position == here, lane_sum[t], taps_grad)
    small_ref[...] = jnp.where(
        position == TAPS, jnp.sum(sums_one[...], axis=1, keepdims=True), taps_grad
    )

    def exchange(chain, s, value):
        small_out[chain, s] = value
        return pair(
            18 + 4 * steps + chain * steps + s,
            small_out.at[chain, s],
            small_in.at[chain, s],
            {"rows": partners[s]},
        )

    step = exchange(0, 0, small_ref[...])
    finals(BRANCH, 1)
    edges_wait(*halos, halo_in, grad_pad)

    @pl.loop(0, groups)
    def _(g):
        group = pl.ds(pl.multiple_of(8 * g, 8), 8)
        taps = taps_ref[group, :]
        sums = [None] * height
        for v in range(KSIZE):
            shifts = [shifted(grad_pad[r, group, :], v - 3) for r in range(height + 6)]
            for u in range(KSIZE):
                t = u * PITCH + v
                tap = jnp.broadcast_to(taps[:, t : t + 1], taps.shape)
                for r in range(height):
                    term = tap * shifts[r + 6 - u]
                    sums[r] = term if sums[r] is None else sums[r] + term
        total = jnp.stack([sums[r] + cotan[r, group, :] for r in range(height)])
        image_grad_ref[group] = jnp.swapaxes(total, 0, 1).astype(bf16)

    for h in range(CUTS):
        pieces(BRANCH, h)

    @pl.loop(0, height)
    def _(r):
        branch = piece_in[BRANCH, r].astype(f32)
        sums_two[...] += branch * cotan[r]
        running[r] = padded[r + 3] + scale * branch

    @pl.loop(0, groups)
    def _(g):
        group = pl.ds(pl.multiple_of(8 * g, 8), 8)
        block_ref[group] = jnp.swapaxes(running[:, group, :], 0, 1).astype(bf16)

    total = jnp.broadcast_to(jnp.sum(sums_two[...], axis=1, keepdims=True), small_ref.shape)
    last = exchange(1, 0, total)
    for s in range(steps):
        for c in range(4):
            row_step(c, s).wait()
            final = s == steps - 1
            a, first = c // 2, c % 2 * (shorter // 16)

            @pl.loop(first, first + shorter // 16)
            def _(i):
                mine = pl.ds(pl.multiple_of(16 * i, 16), 16)
                total = row_out[s, a, mine, :].astype(f32) + row_in[s, a, mine, :].astype(f32)
                if final:
                    grads_ref[a][mine, :] = total
                else:
                    row_out[s + 1, a, mine, :] = total.astype(bf16)

            if not final:
                row_step(c, s + 1).start()

    small = small_ref[...]
    for s in range(steps):
        step.wait()
        small = small + small_in[0, s]
        if s + 1 < steps:
            step = exchange(0, s + 1, small)
    for s in range(steps):
        last.wait()
        total = total + small_in[1, s]
        if s + 1 < steps:
            last = exchange(1, s + 1, total)
    square[0:channels] = jnp.where(position == TAPS + 1, total, small)
    turned = square[...].T
    for u in range(PITCH):
        packed_ref[u] = turned[u * PITCH : (u + 1) * PITCH, 0:channels]

    for a in range(2):
        for h in range(CUTS):

            @pl.loop(0, planes)
            def _(p):
                @pl.when(p > plane)
                def _():
                    sum_copy(a, h, p, 0).wait_send()

                @pl.when(p < plane)
                def _():
                    sum_copy(a, h, p, 1).wait_send()


def run_block(n, arrays):
    f32, bf16 = jnp.float32, jnp.bfloat16
    channels, height, breadth = arrays[0].shape
    hidden, width = arrays[5].shape
    planes = n // GROUP
    part = height // GROUP
    pc = part // CUTS
    every = GROUP * hidden
    pixels = pc * breadth
    rows = lax.axis_size("rows")
    steps = rows.bit_length() - 1
    pairs = 18 + 6 * steps
    vmem = pl.BlockSpec(memory_space=pltpu.VMEM)
    dma = pltpu.SemaphoreType.DMA
    return pl.pallas_call(
        functools.partial(block_kernel, n, rows),
        out_shape=(
            jax.ShapeDtypeStruct((channels, height, breadth), bf16),
            jax.ShapeDtypeStruct((channels, height, breadth), bf16),
            jax.ShapeDtypeStruct((PITCH, PITCH, channels), f32),
            jax.ShapeDtypeStruct((hidden, width), f32),
            jax.ShapeDtypeStruct((hidden, width), f32),
        ),
        in_specs=[pl.BlockSpec(memory_space=pl.ANY)] * 7,
        out_specs=(vmem,) * 5,
        scratch_shapes=[
            pltpu.VMEM((channels, height, breadth), bf16),
            pltpu.VMEM((channels, height, breadth), bf16),
            pltpu.VMEM((KSIZE, KSIZE, channels), f32),
            pltpu.VMEM((1, channels), f32),
            pltpu.VMEM((1, channels), f32),
            pltpu.VMEM((128, 128), f32),
            pltpu.VMEM((channels, 128), f32),
            pltpu.VMEM((channels, 128), f32),
            pltpu.VMEM((height, channels, breadth), f32),
            pltpu.VMEM((2, 3, channels, breadth), bf16),
            pltpu.VMEM((height + 6, channels, breadth), f32),
            pltpu.VMEM((height, channels, breadth), f32),
            pltpu.VMEM((2, height, channels, breadth), bf16),
            pltpu.VMEM((2, CUTS, n, pc, channels, breadth), bf16),
            pltpu.VMEM((1, 128), f32),
            pltpu.VMEM((n, 1, 128), f32),
            pltpu.VMEM((n, channels, breadth), f32),
            pltpu.VMEM((2, every, width), bf16),
            pltpu.VMEM((2, width, every), bf16),
            pltpu.VMEM((2, CUTS, width, pixels), bf16),
            pltpu.VMEM((CUTS, every, pixels), f32),
            pltpu.VMEM((every, pixels), f32),
            pltpu.VMEM((2, CUTS, every, pixels), bf16),
            pltpu.VMEM((2, CUTS, planes, GROUP, pc, channels, breadth), f32),
            pltpu.VMEM((2, CUTS, planes, GROUP, pc, channels, breadth), bf16),
            pltpu.VMEM((2, CUTS, planes + 1, GROUP, pc, channels, breadth), bf16),
            pltpu.VMEM((2, height, channels, breadth), bf16),
            pltpu.VMEM((part, 4, breadth), f32),
            pltpu.VMEM((planes, part, 4, breadth), f32),
            pltpu.VMEM((height, 4, breadth), f32),
            pltpu.VMEM((2, 2 * hidden, width), f32),
            pltpu.VMEM((2, 2 * hidden, width), bf16),
            pltpu.VMEM((2, 2 * hidden, width), bf16),
            pltpu.VMEM((2, hidden, width), bf16),
            pltpu.VMEM((2, hidden, width), bf16),
            pltpu.VMEM((steps, 2, hidden, width), bf16),
            pltpu.VMEM((steps, 2, hidden, width), bf16),
            pltpu.VMEM((height + 6, channels, breadth), f32),
            pltpu.VMEM((channels, breadth), f32),
            pltpu.VMEM((channels, breadth), f32),
            pltpu.VMEM((KSIZE * KSIZE, channels, breadth), f32),
            pltpu.VMEM((2, 3, channels, breadth), bf16),
            pltpu.VMEM((2, 3, channels, breadth), bf16),
            pltpu.VMEM((2, 3, channels, breadth), bf16),
            pltpu.VMEM((2, steps, channels, 128), f32),
            pltpu.VMEM((2, steps, channels, 128), f32),
            dma((7,)),
            dma((2, CUTS, GROUP)),
            dma((2, GROUP)),
            dma((2, CUTS, 2, n)),
            dma((2, CUTS, n)),
            dma((n,)),
            dma((n,)),
            dma((2, CUTS, planes)),
            dma((2, CUTS, planes + 1)),
            dma((2, CUTS, GROUP)),
            dma((2, CUTS, GROUP)),
            dma((CUTS, planes)),
            dma((CUTS, planes)),
            dma((CUTS, GROUP)),
            dma((CUTS, GROUP)),
            dma((pairs,)),
            dma((pairs,)),
        ],
        compiler_params=pltpu.CompilerParams(
            collective_id=0, has_side_effects=True, vmem_limit_bytes=40 * 2**20
        ),
        cost_estimate=pl.CostEstimate(
            flops=4000000000, bytes_accessed=10000000, transcendentals=0
        ),
    )(*arrays)


def body(image, dw_kernel, ln_gain, w_in, w_out, layer_scale, cotangent):
    n = lax.axis_size("chan")
    block_out, image_grad, packed, grad_in, grad_out = run_block(
        n,
        (
            *[
                pltpu.with_memory_space_constraint(value, pltpu.HBM)
                for value in (
                    image[:, 0],
                    cotangent[:, 0],
                    jnp.transpose(dw_kernel, (1, 2, 0)),
                    ln_gain[None, :],
                    layer_scale[None, :],
                    w_in.T,
                    w_out,
                )
            ],
        ),
    )
    return (
        block_out[:, None],
        image_grad[:, None],
        jnp.transpose(packed[:KSIZE, :KSIZE], (2, 0, 1)),
        packed[KSIZE, 0],
        packed[KSIZE, 1],
        grad_in.T,
        grad_out,
    )


def solution(mesh):
    return jax.shard_map(
        body,
        mesh=mesh,
        in_specs=(
            P("chan", None, "rows", None),
            P("chan", None, None),
            P("chan"),
            P(None, "chan"),
            P("chan", None),
            P("chan"),
            P("chan", None, "rows", None),
        ),
        out_specs=(
            P("chan", None, "rows", None),
            P("chan", None, "rows", None),
            P("chan", None, None),
            P("chan"),
            P("chan"),
            P(None, "chan"),
            P("chan", None),
        ),
        check_vma=False,
    )
```
